32 devices in a mesh: lon: 16 (over z, y, core), lat: 2 (over x).
Axes of the slice: x: 2, y: 2, z: 4, core: 2. Of those that a mesh axis runs over, the one named last changes fastest.
Arguments:
- field: bfloat16 [1, 64, 256, 256], P(None, 'lat', 'lon'), may hold values from -6 to 6
- depth_kernel: float32 [7, 7, 256], replicated, may hold values from -0.875 to 0.875
- layer_norm_gain: float32 [256], replicated, may hold values from 0.1 to 1.9
- inner_weight: bfloat16 [256, 1024], replicated, may hold values from -0.375 to 0.375
- outer_weight: bfloat16 [1024, 256], replicated, may hold values from -0.1875 to 0.1875
- layer_scale: float32 [256], replicated, may hold values from 0.3 to 1.5
- down_weight: bfloat16 [1024, 512], replicated, may hold values from -0.1875 to 0.1875
- cotangent: bfloat16 [1, 32, 128, 512], P(None, 'lat', 'lon'), may hold values from -6 to 6
Outputs:
- coarse: bfloat16 [1, 32, 128, 512], P(None, 'lat', 'lon')
- grad_field: bfloat16 [1, 64, 256, 256], P(None, 'lat', 'lon')
- grad_kernel: float32 [7, 7, 256], replicated
- grad_gain: float32 [256], replicated
- grad_inner: float32 [256, 1024], replicated
- grad_outer: float32 [1024, 256], replicated
- grad_scale: float32 [256], replicated
- grad_down: float32 [1024, 512], replicated
The draws below stay inside these ranges and needn't reach their ends.
All inputs are finite; a program needn't handle non-finite values.
Results may differ from the reference program's by a relative error of at most 0.0071.
Values may be sent and summed in bfloat16 or wider, within the bound.
A program may use at most 64 MiB of HBM per device.

```python
import math
from functools import partial
import jax
import jax.numpy as jnp
from jax import lax

CH = 256
HIDDEN_SIZE = 1024
COUT = 512
BATCH = 1
NLAT = 64
NLON = 256
PARAMS = 1061632


def level_of(rng, dims, pieces, low, high):
    gain = 1.0
    for dim, blocks in pieces:
        draws = jax.random.uniform(jax.random.fold_in(jax.random.fold_in(rng, 6), dim), (blocks,), jnp.float32, low / len(pieces), high / len(pieces))
        gain = gain * jnp.repeat(jnp.exp(draws), dims[dim] // blocks).reshape((-1,) + (1,) * (len(dims) - 1 - dim))
    return gain


def noise(stream_key, dims, scale, most, shards=(), held_as=jnp.bfloat16):
    values = scale * jax.random.normal(stream_key, dims, jnp.float32)
    if shards:
        values = values * level_of(stream_key, dims, shards, -0.22, 0.18)
    return jnp.clip(values, -most, most).astype(held_as)


def setup_inputs(seed: int = 0) -> dict:
    seeds = jax.random.split(jax.random.key(seed), 9)
    return {
        "field": noise(seeds[0], (BATCH, NLAT, NLON, CH), 1.0, 6.0, ((1, 2), (2, 16))),
        "depth_kernel": noise(seeds[1], (7, 7, CH), 49 ** -0.5, 0.875, (), jnp.float32),
        "layer_norm_gain": jnp.clip(1.0 + 0.18 * jax.random.normal(seeds[2], (CH,), jnp.float32), 0.1, 1.9),
        "inner_weight": noise(seeds[3], (CH, HIDDEN_SIZE), CH ** -0.5, 0.375),
        "outer_weight": noise(seeds[4], (HIDDEN_SIZE, CH), HIDDEN_SIZE ** -0.5, 0.1875),
        "layer_scale": jnp.clip(jnp.exp(jax.random.uniform(seeds[5], (CH,), jnp.float32, math.log(0.3), math.log(1.5))), 0.3, 1.5),
        "down_weight": noise(seeds[6], (4 * CH, COUT), (4 * CH) ** -0.5, 0.1875),
        "cotangent": noise(seeds[7], (BATCH, NLAT // 2, NLON // 2, COUT), 1.0, 6.0, ((1, 2), (2, 16))),
    }


EPS = 1e-06

def extend_field(values, width):
    padded = jnp.pad(values, ((0, 0), (width, width), (0, 0), (0, 0)))
    return jnp.concatenate([padded[:, :, -width:], padded, padded[:, :, :width]], axis=2)

def depth_apply(padded, kernel):
    rows = padded.shape[1] - 6
    cols = padded.shape[2] - 6
    total = jnp.zeros((padded.shape[0], rows, cols, padded.shape[3]), jnp.float32)
    for row_shift in range(7):
        for col_shift in range(7):
            total = total + kernel[row_shift, col_shift] * padded[:, row_shift:row_shift + rows, col_shift:col_shift + cols]
    return total

def depth_transpose(padded, kernel):
    rows = padded.shape[1] - 6
    cols = padded.shape[2] - 6
    total = jnp.zeros((padded.shape[0], rows, cols, padded.shape[3]), jnp.float32)
    for row_shift in range(7):
        for col_shift in range(7):
            total = total + kernel[row_shift, col_shift] * padded[:, 6 - row_shift:6 - row_shift + rows, 6 - col_shift:6 - col_shift + cols]
    return total

def kernel_terms(padded, grad):
    rows = grad.shape[1]
    cols = grad.shape[2]
    terms = []
    for row_shift in range(7):
        for col_shift in range(7):
            terms.append(lax.optimization_barrier(jnp.sum(padded[:, row_shift:row_shift + rows, col_shift:col_shift + cols] * grad, axis=(0, 1, 2))))
    return jnp.stack(terms).reshape(7, 7, grad.shape[3])

def to_patches(values):
    batch, rows, cols, channel_count = values.shape
    return values.reshape(batch, rows // 2, 2, cols // 2, 2, channel_count).transpose(0, 1, 3, 2, 4, 5).reshape(-1, 4 * channel_count)

def from_patches(values, shape):
    batch, rows, cols, channel_count = shape
    return values.reshape(batch, rows // 2, cols // 2, 2, 2, channel_count).transpose(0, 1, 3, 2, 4, 5).reshape(batch, rows, cols, channel_count)

def block_pass(padded, grad_coarse, depth_kernel, layer_norm_gain, inner_weight, outer_weight, layer_scale, down_weight):
    inner = padded[:, 3:-3, 3:-3]
    channel_count = inner.shape[3]
    mixed = depth_apply(padded.astype(jnp.float32), depth_kernel)
    centered_input = mixed - lax.optimization_barrier(jnp.mean(mixed, axis=-1, keepdims=True))
    inverse_deviation = lax.rsqrt(lax.optimization_barrier(jnp.mean(centered_input * centered_input, axis=-1, keepdims=True)) + EPS)
    standardized_input = centered_input * inverse_deviation
    normalized_output = (standardized_input * layer_norm_gain).astype(jnp.bfloat16).reshape(-1, channel_count)
    preact = jnp.dot(normalized_output, inner_weight, preferred_element_type=jnp.float32)
    hidden = jax.nn.gelu(preact, approximate=False).astype(jnp.bfloat16)
    branch = jnp.dot(hidden, outer_weight, preferred_element_type=jnp.float32)
    blocked = (inner.astype(jnp.float32).reshape(-1, channel_count) + layer_scale * branch).astype(jnp.bfloat16)
    patches = to_patches(blocked.reshape(inner.shape))
    coarse = jnp.dot(patches, down_weight, preferred_element_type=jnp.float32).astype(jnp.bfloat16)
    coarse = coarse.reshape(grad_coarse.shape[:3] + (down_weight.shape[1],))
    flat_grad = grad_coarse.reshape(-1, down_weight.shape[1])
    raw_down = jnp.dot(patches.T, flat_grad, preferred_element_type=jnp.float32)
    grad_patch = jnp.dot(flat_grad, down_weight.T, preferred_element_type=jnp.float32).astype(jnp.bfloat16)
    grad_blocked = from_patches(grad_patch, inner.shape).reshape(-1, channel_count)
    raw_scale = lax.optimization_barrier(jnp.sum(grad_blocked.astype(jnp.float32) * branch, axis=0))
    grad_branch = (grad_blocked.astype(jnp.float32) * layer_scale).astype(jnp.bfloat16)
    grad_hidden = jnp.dot(grad_branch, outer_weight.T, preferred_element_type=jnp.float32)
    grad_pre = jax.vjp(partial(jax.nn.gelu, approximate=False), preact)[1](grad_hidden)[0].astype(jnp.bfloat16)
    raw_outer = jnp.dot(hidden.T, grad_branch, preferred_element_type=jnp.float32)
    raw_inner = jnp.dot(normalized_output.T, grad_pre, preferred_element_type=jnp.float32)
    normalized_gradient = jnp.dot(grad_pre, inner_weight.T, preferred_element_type=jnp.float32).reshape(mixed.shape)
    unclipped_gain = lax.optimization_barrier(jnp.sum(normalized_gradient * standardized_input, axis=(0, 1, 2)))
    gain_scaled_output = normalized_gradient * layer_norm_gain
    depthwise_gradient = (gain_scaled_output - lax.optimization_barrier(jnp.mean(gain_scaled_output, axis=-1, keepdims=True)) - standardized_input * lax.optimization_barrier(jnp.mean(gain_scaled_output * standardized_input, axis=-1, keepdims=True))) * inverse_deviation
    depthwise_gradient = depthwise_gradient.astype(jnp.bfloat16)
    grad_blocked = grad_blocked.reshape(inner.shape)
    return (coarse, grad_blocked, depthwise_gradient, (unclipped_gain, raw_inner, raw_outer, raw_scale, raw_down))

def reference(field, depth_kernel, layer_norm_gain, inner_weight, outer_weight, layer_scale, down_weight, cotangent):
    total_rows = field.shape[1]
    block_rows = 2 * math.gcd(total_rows // 2, 8)
    count = total_rows // block_rows
    padded_all = extend_field(field, 3)
    starts = jnp.arange(count, dtype=jnp.int32) * block_rows
    channel_count = field.shape[3]
    zeros_first = (jnp.zeros((channel_count,), jnp.float32), jnp.zeros(inner_weight.shape, jnp.float32), jnp.zeros(outer_weight.shape, jnp.float32), jnp.zeros((channel_count,), jnp.float32), jnp.zeros(down_weight.shape, jnp.float32))

    def first_step(carry, start):
        padded = lax.dynamic_slice_in_dim(padded_all, start, block_rows + 6, 1)
        grad_coarse = lax.dynamic_slice_in_dim(cotangent, start // 2, block_rows // 2, 1)
        coarse, grad_blocked, depthwise_gradient, raws = block_pass(padded, grad_coarse, depth_kernel, layer_norm_gain, inner_weight, outer_weight, layer_scale, down_weight)
        carry = tuple((left + right for left, right in zip(carry, raws)))
        return (carry, (coarse, grad_blocked, depthwise_gradient))
    raws, stacked = lax.scan(first_step, zeros_first, starts)

    def join(values):
        moved = jnp.moveaxis(values, 0, 1)
        return moved.reshape((moved.shape[0], moved.shape[1] * moved.shape[2]) + moved.shape[3:])
    coarse = join(stacked[0])
    grad_blocked_all = join(stacked[1])
    grad_depth_all = join(stacked[2])
    grad_padded_all = extend_field(grad_depth_all, 3)

    def second_step(carry, start):
        padded = lax.dynamic_slice_in_dim(padded_all, start, block_rows + 6, 1).astype(jnp.float32)
        grad_padded = lax.dynamic_slice_in_dim(grad_padded_all, start, block_rows + 6, 1).astype(jnp.float32)
        grad_blocked = lax.dynamic_slice_in_dim(grad_blocked_all, start, block_rows, 1)
        spread = depth_transpose(grad_padded, depth_kernel)
        out_rows = (grad_blocked.astype(jnp.float32) + spread).astype(jnp.bfloat16)
        carry = carry + kernel_terms(padded, grad_padded[:, 3:-3, 3:-3])
        return (carry, out_rows)
    raw_kernel, field_rows = lax.scan(second_step, jnp.zeros((7, 7, channel_count), jnp.float32), starts)
    grad_field = join(field_rows)
    unclipped_gain, raw_inner, raw_outer, raw_scale, raw_down = raws
    total = jnp.sum(raw_kernel * raw_kernel) + jnp.sum(unclipped_gain * unclipped_gain) + jnp.sum(raw_inner * raw_inner) + jnp.sum(raw_outer * raw_outer) + jnp.sum(raw_scale * raw_scale) + jnp.sum(raw_down * raw_down)
    factor = jnp.minimum(1.0, math.sqrt(PARAMS) / jnp.sqrt(total + EPS))
    return (coarse, grad_field, raw_kernel * factor, unclipped_gain * factor, raw_inner * factor, raw_outer * factor, raw_scale * factor, raw_down * factor)
```

```python
from functools import partial
import math

import jax
import jax.numpy as jnp
from jax import lax
from jax.experimental import pallas as pl
from jax.experimental.pallas import tpu as pltpu
from jax.sharding import PartitionSpec as P

PARAMS = 1061632


EPS = 1e-06


def padded_2(cells, sides, width, closed):
    for axis, dim in sides:
        count = lax.axis_size(axis)
        ends = count if closed else count - 1
        head = lax.slice_in_dim(cells, 0, width, axis=dim)
        tail = lax.slice_in_dim(cells, cells.shape[dim] - width, cells.shape[dim], axis=dim)
        cells = jnp.concatenate(
            [
                lax.ppermute(tail, axis, [(i, (i + 1) % count) for i in range(ends)]),
                cells,
                lax.ppermute(head, axis, [((i + 1) % count, i) for i in range(ends)]),
            ],
            axis=dim,
        )
    return cells


def depth_apply(padded, kernel):
    rows = padded.shape[1] - 6
    cols = padded.shape[2] - 6
    total = jnp.zeros((padded.shape[0], rows, cols, padded.shape[3]), jnp.float32)
    for row_shift in range(7):
        for col_shift in range(7):
            total = (
                total
                + kernel[row_shift, col_shift]
                * padded[:, row_shift : row_shift + rows, col_shift : col_shift + cols]
            )
    return total


def depth_transpose(padded, kernel):
    rows = padded.shape[1] - 6
    cols = padded.shape[2] - 6
    total = jnp.zeros((padded.shape[0], rows, cols, padded.shape[3]), jnp.float32)
    for row_shift in range(7):
        for col_shift in range(7):
            total = (
                total
                + kernel[row_shift, col_shift]
                * padded[
                    :, 6 - row_shift : 6 - row_shift + rows, 6 - col_shift : 6 - col_shift + cols
                ]
            )
    return total


def kernel_terms(padded, grad):
    rows = grad.shape[1]
    cols = grad.shape[2]
    terms = []
    for row_shift in range(7):
        for col_shift in range(7):
            terms.append(
                jnp.sum(
                    padded[:, row_shift : row_shift + rows, col_shift : col_shift + cols] * grad,
                    axis=(0, 1, 2),
                )
            )
    return jnp.stack(terms).reshape(7, 7, grad.shape[3])


def to_patches(values):
    batch, rows, cols, channel_count = values.shape
    return (
        values.reshape(batch, rows // 2, 2, cols // 2, 2, channel_count)
        .transpose(0, 1, 3, 2, 4, 5)
        .reshape(-1, 4 * channel_count)
    )


def from_patches(values, shape):
    batch, rows, cols, channel_count = shape
    return (
        values.reshape(batch, rows // 2, cols // 2, 2, 2, channel_count)
        .transpose(0, 1, 3, 2, 4, 5)
        .reshape(batch, rows, cols, channel_count)
    )


MESH = pl.DeviceIdType.MESH


def place(mesh_shape):
    lon_bits = mesh_shape["lon"].bit_length() - 1
    lat_bits = mesh_shape["lat"].bit_length() - 1
    core = ("lon", 0)
    groups = [
        [("lat", k) for k in range(lat_bits)],
        [("lon", k) for k in range(1, min(2, lon_bits))],
        [("lon", k) for k in range(2, lon_bits)],
    ]
    orders = []
    for p in range(3):
        rotated = groups[p:] + groups[:p]
        orders.append([core] + [bit for group in rotated for bit in group])
    devices = mesh_shape["lon"] * mesh_shape["lat"]
    unit = 3 * 16 * devices
    rows = -(-(4096 + 64) // unit) * unit
    return orders, rows, devices


def partner_of(bit):
    axis, k = bit
    me = lax.axis_index(axis)
    b = lax.rem(lax.div(me, 2**k), 2)
    return b, {axis: me + (1 - 2 * b) * 2**k}


def sum_kernel_body(orders, devices, inner, outer, down, small, out, acc, send, recv, ssem, rsem):
    rows = acc.shape[0]
    part_rows = rows // 3
    stages = len(orders[0])
    barrier = pltpu.get_barrier_semaphore()
    for bit in orders[0]:
        _, device = partner_of(bit)
        pl.semaphore_signal(barrier, inc=1, device_id=device, device_id_type=MESH)

    def pack_inner(i, carry):
        r = pl.multiple_of(i * 64, 64)
        for c in range(4):
            acc[pl.ds(c * 256 + r, 64), :] = inner[pl.ds(r, 64), c * 256 : (c + 1) * 256]
        return carry

    lax.fori_loop(0, 4, pack_inner, 0)

    def pack_rest(i, carry):
        r = pl.multiple_of(i * 64, 64)
        acc[pl.ds(1024 + r, 64), :] = outer[pl.ds(r, 64), :]
        acc[pl.ds(2048 + r, 64), :] = down[pl.ds(r, 64), 0:256]
        acc[pl.ds(3072 + r, 64), :] = down[pl.ds(r, 64), 256:512]
        return carry

    lax.fori_loop(0, 16, pack_rest, 0)
    acc[4096:4160, :] = small[...]

    def clear(i, carry):
        acc[pl.ds(pl.multiple_of(4160 + i * 32, 32), 32), :] = jnp.zeros((32, 256), jnp.float32)
        return carry

    lax.fori_loop(0, (rows - 4160) // 32, clear, 0)
    pl.semaphore_wait(barrier, stages)

    unit = part_rows // devices
    offs = [p * part_rows for p in range(3)]
    keeps = [[None] * stages for _ in range(3)]
    sent = []

    def start(s, p):
        b, device = partner_of(orders[p][s])
        half = part_rows >> (s + 1)
        base = p * part_rows + part_rows - 2 * half
        away = offs[p] + (1 - b) * half
        keeps[p][s] = offs[p] + b * half
        chunk = min(half, 4 * unit)

        def cast(i, carry):
            r = i * chunk
            send[pl.ds(pl.multiple_of(base + r, 16), chunk), :] = acc[
                pl.ds(pl.multiple_of(away + r, 16), chunk), :
            ].astype(jnp.bfloat16)
            return carry

        lax.fori_loop(0, half // chunk, cast, 0)
        copy = pltpu.make_async_remote_copy(
            src_ref=send.at[pl.ds(base, half)],
            dst_ref=recv.at[pl.ds(base, half)],
            send_sem=ssem.at[p, s],
            recv_sem=rsem.at[p, s],
            device_id=device,
            device_id_type=MESH,
        )
        copy.start()
        sent.append(copy)
        return copy

    def finish(s, p, copy):
        half = part_rows >> (s + 1)
        base = p * part_rows + part_rows - 2 * half
        keep = keeps[p][s]
        chunk = min(half, 4 * unit)
        copy.wait_recv()

        def add(i, carry):
            r = i * chunk
            mine = pl.ds(pl.multiple_of(keep + r, 16), chunk)
            acc[mine, :] = acc[mine, :] + recv[
                pl.ds(pl.multiple_of(base + r, 16), chunk), :
            ].astype(jnp.float32)
            return carry

        lax.fori_loop(0, half // chunk, add, 0)
        offs[p] = keep

    def spread(s, p):
        _, device = partner_of(orders[p][s])
        half = part_rows >> (s + 1)
        mine = pl.ds(pl.multiple_of(keeps[p][s], 16), half)
        copy = pltpu.make_async_remote_copy(
            src_ref=out.at[mine],
            dst_ref=out.at[mine],
            send_sem=ssem.at[p, stages + s],
            recv_sem=rsem.at[p, stages + s],
            device_id=device,
            device_id_type=MESH,
        )
        copy.start()
        sent.append(copy)
        return copy

    flight = [start(0, p) for p in range(3)]
    for s in range(stages):
        for p in range(3):
            finish(s, p, flight[p])
            if s + 1 < stages:
                flight[p] = start(s + 1, p)
            else:
                mine = pl.ds(pl.multiple_of(offs[p], 16), unit)
                out[mine, :] = acc[mine, :].astype(jnp.bfloat16)
                flight[p] = spread(stages - 1, p)
    for s in range(stages - 2, -1, -1):
        for p in range(3):
            flight[p].wait_recv()
            flight[p] = spread(s, p)
    for p in range(3):
        flight[p].wait_recv()
    for copy in sent:
        copy.wait_send()


def summed(inner, outer, down, small, mesh_shape):
    orders, rows, devices = place(mesh_shape)
    stages = len(orders[0])
    vmem = pl.BlockSpec(memory_space=pltpu.VMEM)
    return pl.pallas_call(
        partial(sum_kernel_body, orders, devices),
        name="sum_gradients",
        out_shape=jax.ShapeDtypeStruct((rows, 256), jnp.bfloat16),
        in_specs=[vmem] * 4,
        out_specs=vmem,
        scratch_shapes=[
            pltpu.VMEM((rows, 256), jnp.float32),
            pltpu.VMEM((rows, 256), jnp.bfloat16),
            pltpu.VMEM((rows, 256), jnp.bfloat16),
            pltpu.SemaphoreType.DMA((3, 2 * stages)),
            pltpu.SemaphoreType.DMA((3, 2 * stages)),
        ],
        compiler_params=pltpu.CompilerParams(
            collective_id=1, has_side_effects=True, vmem_limit_bytes=48 << 20
        ),
    )(inner, outer, down, small)


def clip_body(sums, inner, outer, down, small):
    def squares(i, total):
        v = sums[pl.ds(pl.multiple_of(i * 64, 64), 64), :].astype(jnp.float32)
        v = v * v
        for width in (32, 16, 8):
            v = v[:width] + v[width:]
        return total + v

    total = jnp.sum(lax.fori_loop(0, 65, squares, jnp.zeros((8, 256), jnp.float32)))
    total = jnp.full((1, 256), total, jnp.float32)
    factor = jnp.minimum(1.0, math.sqrt(PARAMS) / jnp.sqrt(total + EPS))

    def write_inner(i, carry):
        r = pl.multiple_of(i * 64, 64)
        for c in range(4):
            inner[pl.ds(r, 64), c * 256 : (c + 1) * 256] = (
                sums[pl.ds(c * 256 + r, 64), :].astype(jnp.float32) * factor
            )
        return carry

    lax.fori_loop(0, 4, write_inner, 0)

    def write_rest(i, carry):
        r = pl.multiple_of(i * 64, 64)
        outer[pl.ds(r, 64), :] = sums[pl.ds(1024 + r, 64), :].astype(jnp.float32) * factor
        down[pl.ds(r, 64), 0:256] = sums[pl.ds(2048 + r, 64), :].astype(jnp.float32) * factor
        down[pl.ds(r, 64), 256:512] = sums[pl.ds(3072 + r, 64), :].astype(jnp.float32) * factor
        return carry

    lax.fori_loop(0, 16, write_rest, 0)
    small[...] = sums[4096:4160, :].astype(jnp.float32) * factor


def clipped(sums):
    vmem = pl.BlockSpec(memory_space=pltpu.VMEM)
    shapes = ((256, 1024), (1024, 256), (1024, 512), (64, 256))
    return pl.pallas_call(
        clip_body,
        name="clip_gradients",
        out_shape=[jax.ShapeDtypeStruct(shape, jnp.float32) for shape in shapes],
        in_specs=[vmem],
        out_specs=[vmem] * 4,
        compiler_params=pltpu.CompilerParams(vmem_limit_bytes=48 << 20),
    )(sums)


def body(
    mesh_shape,
    field,
    depth_kernel,
    layer_norm_gain,
    inner_weight,
    outer_weight,
    layer_scale,
    down_weight,
    cotangent,
):
    channel_count = field.shape[3]
    wide = padded_2(field, (("lon", 2),), 3, True)
    padded = padded_2(wide, (("lat", 1),), 3, False)
    mixed = depth_apply(padded.astype(jnp.float32), depth_kernel)
    centered_input = mixed - jnp.mean(mixed, axis=-1, keepdims=True)
    inverse_deviation = lax.rsqrt(
        jnp.mean(centered_input * centered_input, axis=-1, keepdims=True) + EPS
    )
    standardized_input = centered_input * inverse_deviation
    normalized_output = (
        (standardized_input * layer_norm_gain).astype(jnp.bfloat16).reshape(-1, channel_count)
    )
    preact = jnp.dot(normalized_output, inner_weight, preferred_element_type=jnp.float32)
    hidden = jax.nn.gelu(preact, approximate=False).astype(jnp.bfloat16)
    branch = jnp.dot(hidden, outer_weight, preferred_element_type=jnp.float32)
    blocked = (field.astype(jnp.float32).reshape(-1, channel_count) + layer_scale * branch).astype(
        jnp.bfloat16
    )
    patches = to_patches(blocked.reshape(field.shape))
    coarse = jnp.dot(patches, down_weight, preferred_element_type=jnp.float32).astype(jnp.bfloat16)
    coarse = coarse.reshape(cotangent.shape)
    flat_grad = cotangent.reshape(-1, cotangent.shape[3])
    raw_down = jnp.dot(patches.T, flat_grad, preferred_element_type=jnp.float32)
    grad_patch = jnp.dot(flat_grad, down_weight.T, preferred_element_type=jnp.float32).astype(
        jnp.bfloat16
    )
    grad_blocked = from_patches(grad_patch, field.shape).reshape(-1, channel_count)
    raw_scale = jnp.sum(grad_blocked.astype(jnp.float32) * branch, axis=0)
    grad_branch = (grad_blocked.astype(jnp.float32) * layer_scale).astype(jnp.bfloat16)
    grad_hidden = jnp.dot(grad_branch, outer_weight.T, preferred_element_type=jnp.float32)
    grad_pre = jax.vjp(partial(jax.nn.gelu, approximate=False), preact)[1](grad_hidden)[0].astype(
        jnp.bfloat16
    )
    raw_outer = jnp.dot(hidden.T, grad_branch, preferred_element_type=jnp.float32)
    raw_inner = jnp.dot(normalized_output.T, grad_pre, preferred_element_type=jnp.float32)
    normalized_gradient = jnp.dot(
        grad_pre, inner_weight.T, preferred_element_type=jnp.float32
    ).reshape(mixed.shape)
    unclipped_gain = jnp.sum(normalized_gradient * standardized_input, axis=(0, 1, 2))
    gain_scaled_output = normalized_gradient * layer_norm_gain
    depthwise_gradient = (
        gain_scaled_output
        - jnp.mean(gain_scaled_output, axis=-1, keepdims=True)
        - standardized_input
        * jnp.mean(gain_scaled_output * standardized_input, axis=-1, keepdims=True)
    ) * inverse_deviation
    depthwise_gradient = depthwise_gradient.astype(jnp.bfloat16)
    grad_wide = padded_2(depthwise_gradient, (("lon", 2),), 3, True)
    grad_padded = padded_2(grad_wide, (("lat", 1),), 3, False).astype(jnp.float32)
    spread = depth_transpose(grad_padded, depth_kernel)
    grad_field = (grad_blocked.reshape(field.shape).astype(jnp.float32) + spread).astype(
        jnp.bfloat16
    )
    raw_kernel = kernel_terms(padded.astype(jnp.float32), depthwise_gradient.astype(jnp.float32))
    small = jnp.concatenate(
        [
            raw_kernel.reshape(49, channel_count),
            unclipped_gain[None],
            raw_scale[None],
            jnp.zeros((13, channel_count), jnp.float32),
        ]
    )
    sums = summed(raw_inner, raw_outer, raw_down, small, mesh_shape)
    grad_inner, grad_outer, grad_down, grad_small = clipped(sums)
    grad_kernel = grad_small[:49].reshape(7, 7, channel_count)
    grad_gain = grad_small[49]
    grad_scale = grad_small[50]
    return (
        coarse,
        grad_field,
        grad_kernel,
        grad_gain,
        grad_inner,
        grad_outer,
        grad_scale,
        grad_down,
    )


def solution(mesh):
    return jax.shard_map(
        partial(body, dict(mesh.shape)),
        mesh=mesh,
        in_specs=(
            P(None, "lat", "lon", None),
            P(),
            P(),
            P(),
            P(),
            P(),
            P(),
            P(None, "lat", "lon", None),
        ),
        out_specs=(
            P(None, "lat", "lon", None),
            P(None, "lat", "lon", None),
            P(),
            P(),
            P(),
            P(),
            P(),
            P(),
        ),
        check_vma=False,
    )
```

```python
from functools import partial
import math

import jax
import jax.numpy as jnp
from jax import lax
from jax.experimental import pallas as pl
from jax.experimental.pallas import tpu as pltpu
from jax.sharding import PartitionSpec as P

PARAMS = 1061632


EPS = 1e-06


MESH = pl.DeviceIdType.MESH


def exchange_copies(edges, cells, side, ends, corner, ssem, rsem, sizes):
    lon, lat = lax.axis_index("lon"), lax.axis_index("lat")
    nlon, _ = sizes
    rows = cells.shape[0]
    left = lax.rem(lon + nlon - 1, nlon)
    right = lax.rem(lon + 1, nlon)

    def copy(src, dst, n, where):
        return pltpu.make_async_remote_copy(
            src_ref=src,
            dst_ref=dst,
            send_sem=ssem.at[n],
            recv_sem=rsem.at[n],
            device_id=where,
            device_id_type=MESH,
        )

    across = [
        copy(edges.at[0:3], side.at[1], 0, {"lon": left, "lat": lat}),
        copy(edges.at[3:6], side.at[0], 1, {"lon": right, "lat": lat}),
    ]
    above = lat - 1
    below = lat + 1
    up = [
        copy(cells.at[0:3], ends.at[1], 2, {"lon": lon, "lat": above}),
        copy(edges.at[0:3, 0:16], corner.at[1, 1], 3, {"lon": left, "lat": above}),
        copy(edges.at[3:6, 0:16], corner.at[1, 0], 4, {"lon": right, "lat": above}),
    ]
    down = [
        copy(cells.at[rows - 3 : rows], ends.at[0], 5, {"lon": lon, "lat": below}),
        copy(edges.at[0:3, rows - 16 : rows], corner.at[0, 1], 6, {"lon": left, "lat": below}),
        copy(edges.at[3:6, rows - 16 : rows], corner.at[0, 0], 7, {"lon": right, "lat": below}),
    ]
    return across, up, down


def greet(barrier, sizes):
    lon, lat = lax.axis_index("lon"), lax.axis_index("lat")
    nlon, nlat = sizes
    left = lax.rem(lon + nlon - 1, nlon)
    right = lax.rem(lon + 1, nlon)

    def signal(where):
        pl.semaphore_signal(barrier, inc=1, device_id=where, device_id_type=MESH)

    signal({"lon": left, "lat": lat})
    signal({"lon": right, "lat": lat})
    for there, ok in ((lat - 1, lat > 0), (lat + 1, lat < nlat - 1)):

        @pl.when(ok)
        def _():
            for other in (left, lon, right):
                signal({"lon": other, "lat": there})


def await_greetings(barrier, sizes, extra):
    lat = lax.axis_index("lat")
    beside = jnp.minimum(lat, 1) + jnp.minimum(sizes[1] - 1 - lat, 1)
    pl.semaphore_wait(barrier, 2 + extra + 3 * beside)


def exchange_start(edges, cells, side, ends, corner, ssem, rsem, sizes):
    lat = lax.axis_index("lat")
    across, up, down = exchange_copies(edges, cells, side, ends, corner, ssem, rsem, sizes)
    for c in across:
        c.start()

    @pl.when(lat > 0)
    def _():
        for c in up:
            c.start()

    @pl.when(lat < sizes[1] - 1)
    def _():
        for c in down:
            c.start()


def exchange_finish(edges, cells, side, ends, corner, ssem, rsem, sizes):
    lat = lax.axis_index("lat")
    across, up, down = exchange_copies(edges, cells, side, ends, corner, ssem, rsem, sizes)
    for c in across:
        c.wait()

    @pl.when(lat > 0)
    def _():
        for sent, came in zip(up, down):
            sent.wait_send()
            came.wait_recv()

    @pl.when(lat < sizes[1] - 1)
    def _():
        for sent, came in zip(down, up):
            sent.wait_send()
            came.wait_recv()

    @pl.when(lat == 0)
    def _():
        ends[0] = jnp.zeros(ends.shape[1:], ends.dtype)
        corner[0] = jnp.zeros(corner.shape[1:], corner.dtype)

    @pl.when(lat == sizes[1] - 1)
    def _():
        ends[1] = jnp.zeros(ends.shape[1:], ends.dtype)
        corner[1] = jnp.zeros(corner.shape[1:], corner.dtype)


def halo_body(sizes, edges, cells, side, ends, corner, ssem, rsem):
    barrier = pltpu.get_barrier_semaphore()
    greet(barrier, sizes)
    await_greetings(barrier, sizes, 0)
    exchange_start(edges, cells, side, ends, corner, ssem, rsem, sizes)
    exchange_finish(edges, cells, side, ends, corner, ssem, rsem, sizes)


def halo_shapes(cells):
    rows, cols, channels = cells.shape
    return [
        jax.ShapeDtypeStruct((2, 3, rows, channels), jnp.bfloat16),
        jax.ShapeDtypeStruct((2, 3, cols, channels), jnp.bfloat16),
        jax.ShapeDtypeStruct((2, 2, 3, 16, channels), jnp.bfloat16),
    ]


HALVES = (slice(0, 128), slice(128, 256))
VMEM_SPEC = pl.BlockSpec(memory_space=pltpu.VMEM)


def halo(edges, cells, mesh_shape):
    return pl.pallas_call(
        partial(halo_body, (mesh_shape["lon"], mesh_shape["lat"])),
        name="field_halo",
        out_shape=halo_shapes(cells),
        in_specs=[VMEM_SPEC] * 2,
        out_specs=[VMEM_SPEC] * 3,
        scratch_shapes=[pltpu.SemaphoreType.DMA((8,)), pltpu.SemaphoreType.DMA((8,))],
        compiler_params=pltpu.CompilerParams(
            collective_id=0, has_side_effects=True, vmem_limit_bytes=8 << 20
        ),
    )(edges, cells)


def extend(cells, side, ends, corner, wide, shifted):
    rows, cols, _ = cells.shape
    f32 = jnp.float32

    def put(where, values):
        values = values.astype(f32)
        for h in range(2):
            wide[h, where, :] = values[:, HALVES[h]]

    def fill(r, carry):
        put(pl.ds(pl.multiple_of((3 + r) * 32 + 8, 8), cols), cells[r])
        return carry

    lax.fori_loop(0, rows, fill, 0)
    for r in range(3):
        put(pl.ds(r * 32 + 8, cols), ends[0, r])
        put(pl.ds((rows + 3 + r) * 32 + 8, cols), ends[1, r])
    for h in range(2):
        for s, first in ((0, 5), (1, 8 + cols)):
            for c in range(3):
                column = first + c
                wide[h, pl.ds(3 * 32 + column, rows, stride=32), :] = side[
                    s, c, :, HALVES[h]
                ].astype(f32)
    for s, first in ((0, 5), (1, 8 + cols)):
        for c in range(3):
            high = corner[0, s, c].astype(f32)
            low = corner[1, s, c].astype(f32)
            for r in range(3):
                put(pl.ds(r * 32 + first + c, 1), high[13 + r : 14 + r])
                put(pl.ds((rows + 3 + r) * 32 + first + c, 1), low[r : r + 1])

    def shift(r, carry):
        for h in range(2):
            v = wide[h, pl.ds(pl.multiple_of(r * 32, 32), 32), :]
            for q in range(7):
                shifted[q, r, :, HALVES[h]] = pltpu.roll(v, 27 - q, 0)[:cols]
        return carry

    lax.fori_loop(0, rows + 6, shift, 0)


def spread_rows(shifted, kernel, first, count, flip):
    total = None
    for q in range(7):
        for p in range(7):
            at = (6 - p) * 7 + (6 - q) if flip else p * 7 + q
            term = shifted[q, pl.ds(first + p, count)] * kernel[at : at + 1, :]
            total = term if total is None else total + term
    return total


def dot(a, b, contract):
    return lax.dot_general(a, b, ((contract[0:1], contract[1:2]), ((), ())), preferred_element_type=jnp.float32)


def block_body(
    cells, side, ends, corner, kernel, gain, inner, outer, scale, down, cotangent,
    coarse, grad_cells, grad_depth, grad_edges, raw_inner, raw_outer, raw_down, small,
    wide, shifted, mixed, grad_wide, blocked, normed, hidden, grad_pre, grad_branch, terms,
):
    rows, cols, channels = cells.shape
    f32, bf16 = jnp.float32, jnp.bfloat16
    cot = cotangent[...]
    pair = cols // 2
    for p in range(2):
        for q in range(2):
            at = (2 * p + q) * channels
            gp = dot(cot, down[at : at + channels, :], (1, 1)).astype(bf16).astype(f32)
            for i in range(rows // 2):
                first = (2 * i + p) * cols + q
                for lane in range(2):
                    grad_wide[lane, pl.ds(first, pair, stride=2), :] = gp[i * pair : (i + 1) * pair, HALVES[lane]]

    extend(cells, side, ends, corner, wide, shifted)

    def convolve(t, carry):
        first = t * 8
        out = spread_rows(shifted, kernel, first, 8, False)
        mixed[pl.ds(pl.multiple_of(first * cols, 128), 8 * cols), :] = out.reshape(8 * cols, channels)
        return carry

    lax.fori_loop(0, rows // 8, convolve, 0)

    small[...] = jnp.zeros(small.shape, f32)
    chunk = 16 * cols
    g = gain[...]
    ls = scale[...]

    def step(t, carry):
        raw_gain, raw_scale = carry
        here = pl.ds(pl.multiple_of(t * chunk, chunk), chunk)
        m = mixed[here, :]
        centered = m - jnp.mean(m, axis=-1, keepdims=True)
        inv = lax.rsqrt(jnp.mean(centered * centered, axis=-1, keepdims=True) + EPS)
        xhat = centered * inv
        nrm = (xhat * g).astype(bf16)
        normed[here, :] = nrm
        pre = dot(nrm, inner[...], (1, 0))
        cdf = 0.5 * (1.0 + lax.erf(pre * math.sqrt(0.5)))
        slope = cdf + pre * (jnp.exp(-0.5 * pre * pre) * (1.0 / math.sqrt(2.0 * math.pi)))
        hid = (pre * cdf).astype(bf16)
        hidden[here, :] = hid
        branch = dot(hid, outer[...], (1, 0))
        field = cells[pl.ds(t * 16, 16)].astype(f32).reshape(chunk, channels)
        block_out = (field + ls * branch).astype(bf16).astype(f32)
        for h in range(2):
            blocked[h, here, :] = block_out[:, HALVES[h]]
        gb = jnp.concatenate([grad_wide[h, here, :] for h in range(2)], axis=1)
        grad_cells[here, :] = gb.astype(bf16)
        raw_scale = raw_scale + jnp.sum(gb * branch, axis=0, keepdims=True)
        gbr = (gb * ls).astype(bf16)
        grad_branch[here, :] = gbr
        gp = (dot(gbr, outer[...], (1, 1)) * slope).astype(bf16)
        grad_pre[here, :] = gp
        gn = dot(gp, inner[...], (1, 1))
        raw_gain = raw_gain + jnp.sum(gn * xhat, axis=0, keepdims=True)
        gx = gn * g
        m1 = jnp.mean(gx, axis=-1, keepdims=True)
        m2 = jnp.mean(gx * xhat, axis=-1, keepdims=True)
        gd = ((gx - m1 - xhat * m2) * inv).astype(bf16)
        grad_depth[pl.ds(t * 16, 16)] = gd.reshape(16, cols, channels)
        gd = gd.astype(f32)
        mixed[here, :] = gd
        for h in range(2):
            grad_wide[h, here, :] = gd[:, HALVES[h]]
        return raw_gain, raw_scale

    zero = jnp.zeros((1, channels), f32)
    raw_gain, raw_scale = lax.fori_loop(0, rows // 16, step, (zero, zero))
    small[49:50, :] = raw_gain
    small[50:51, :] = raw_scale
    raw_outer[...] = dot(hidden[...], grad_branch[...], (0, 0))
    raw_inner[...] = dot(normed[...], grad_pre[...], (0, 0))
    total = None
    for p in range(2):
        for q in range(2):
            at = (2 * p + q) * channels
            lanes = []
            for h in range(2):
                lanes.append(
                    jnp.concatenate(
                        [
                            blocked[h, pl.ds((2 * i + p) * cols + q, pair, stride=2), :]
                            for i in range(rows // 2)
                        ]
                    ).astype(bf16)
                )
            patch = jnp.concatenate(lanes, axis=1)
            part = dot(patch, down[at : at + channels, :], (1, 0))
            total = part if total is None else total + part
            raw_down[at : at + channels, :] = dot(patch, cot, (0, 0))
    coarse[...] = total.astype(bf16)

    terms[...] = jnp.zeros(terms.shape, f32)

    def kernel_step(t, carry):
        first = t * 4
        gd = mixed[pl.ds(pl.multiple_of(first * cols, 64), 4 * cols), :].reshape(4, cols, channels)
        for q in range(7):
            for p in range(7):
                prod = shifted[q, pl.ds(first + p, 4)] * gd
                prod = (prod[0] + prod[1]) + (prod[2] + prod[3])
                terms[p * 7 + q] = terms[p * 7 + q] + (prod[0:8] + prod[8:16])
        return carry

    lax.fori_loop(0, rows // 4, kernel_step, 0)
    small[0:49, :] = jnp.sum(terms[...], axis=1)
    for h in range(2):
        for c in range(3):
            for at, column in ((c, c), (3 + c, cols - 3 + c)):
                grad_edges[at, :, HALVES[h]] = grad_wide[
                    h, pl.ds(column, rows, stride=cols), :
                ].astype(bf16)


def block(cells, halos, kernel, gain, inner, outer, scale, down, cotangent):
    rows, cols, channels = cells.shape
    count = rows * cols
    hid = inner.shape[1]
    f32, bf16 = jnp.float32, jnp.bfloat16
    return pl.pallas_call(
        block_body,
        name="block",
        out_shape=[
            jax.ShapeDtypeStruct(cotangent.shape, bf16),
            jax.ShapeDtypeStruct((count, channels), bf16),
            jax.ShapeDtypeStruct(cells.shape, bf16),
            jax.ShapeDtypeStruct((6, rows, channels), bf16),
            jax.ShapeDtypeStruct(inner.shape, f32),
            jax.ShapeDtypeStruct(outer.shape, f32),
            jax.ShapeDtypeStruct(down.shape, f32),
            jax.ShapeDtypeStruct((64, channels), f32),
        ],
        in_specs=[VMEM_SPEC] * 11,
        out_specs=[VMEM_SPEC] * 8,
        scratch_shapes=[
            pltpu.VMEM((2, (rows + 6) * 32, channels // 2), f32),
            pltpu.VMEM((7, rows + 6, cols, channels), f32),
            pltpu.VMEM((count, channels), f32),
            pltpu.VMEM((2, count, channels // 2), f32),
            pltpu.VMEM((2, count, channels // 2), f32),
            pltpu.VMEM((count, channels), bf16),
            pltpu.VMEM((count, hid), bf16),
            pltpu.VMEM((count, hid), bf16),
            pltpu.VMEM((count, channels), bf16),
            pltpu.VMEM((49, 8, channels), f32),
        ],
        compiler_params=pltpu.CompilerParams(vmem_limit_bytes=48 << 20),
    )(cells, *halos, kernel, gain, inner, outer, scale, down, cotangent)


def place(mesh_shape):
    lon_bits = mesh_shape["lon"].bit_length() - 1
    lat_bits = mesh_shape["lat"].bit_length() - 1
    core = ("lon", 0)
    groups = [
        [("lat", k) for k in range(lat_bits)],
        [("lon", k) for k in range(1, min(2, lon_bits))],
        [("lon", k) for k in range(2, lon_bits)],
    ]
    orders = []
    for p in range(3):
        rotated = groups[p:] + groups[:p]
        orders.append([core] + [bit for group in rotated for bit in group])
    devices = mesh_shape["lon"] * mesh_shape["lat"]
    unit = 3 * 16 * devices
    rows = -(-(4096 + 64) // unit) * unit
    return orders, rows, devices


def partner_of(bit):
    axis, k = bit
    me = lax.axis_index(axis)
    b = lax.rem(lax.div(me, 2**k), 2)
    return b, {axis: me + (1 - 2 * b) * 2**k}


def sum_kernel_body(
    orders, devices, sizes, edges, cells, inner, outer, down, small,
    out, side, ends, corner, acc, send, recv, ssem, rsem, halo_ssem, halo_rsem,
):
    rows = acc.shape[0]
    part_rows = rows // 3
    stages = len(orders[0])
    barrier = pltpu.get_barrier_semaphore()
    for bit in orders[0]:
        _, device = partner_of(bit)
        pl.semaphore_signal(barrier, inc=1, device_id=device, device_id_type=MESH)
    greet(barrier, sizes)

    def pack_inner(i, carry):
        r = pl.multiple_of(i * 64, 64)
        for c in range(4):
            acc[pl.ds(c * 256 + r, 64), :] = inner[pl.ds(r, 64), c * 256 : (c + 1) * 256]
        return carry

    lax.fori_loop(0, 4, pack_inner, 0)

    def pack_rest(i, carry):
        r = pl.multiple_of(i * 64, 64)
        acc[pl.ds(1024 + r, 64), :] = outer[pl.ds(r, 64), :]
        acc[pl.ds(2048 + r, 64), :] = down[pl.ds(r, 64), 0:256]
        acc[pl.ds(3072 + r, 64), :] = down[pl.ds(r, 64), 256:512]
        return carry

    lax.fori_loop(0, 16, pack_rest, 0)
    acc[4096:4160, :] = small[...]

    def clear(i, carry):
        acc[pl.ds(pl.multiple_of(4160 + i * 32, 32), 32), :] = jnp.zeros((32, 256), jnp.float32)
        return carry

    lax.fori_loop(0, (rows - 4160) // 32, clear, 0)
    await_greetings(barrier, sizes, stages)
    exchange_start(edges, cells, side, ends, corner, halo_ssem, halo_rsem, sizes)

    unit = part_rows // devices
    offs = [p * part_rows for p in range(3)]
    keeps = [[None] * stages for _ in range(3)]
    sent = []

    def start(s, p):
        b, device = partner_of(orders[p][s])
        half = part_rows >> (s + 1)
        base = p * part_rows + part_rows - 2 * half
        away = offs[p] + (1 - b) * half
        keeps[p][s] = offs[p] + b * half
        chunk = min(half, 4 * unit)

        def cast(i, carry):
            r = i * chunk
            send[pl.ds(pl.multiple_of(base + r, 16), chunk), :] = acc[
                pl.ds(pl.multiple_of(away + r, 16), chunk), :
            ].astype(jnp.bfloat16)
            return carry

        lax.fori_loop(0, half // chunk, cast, 0)
        copy = pltpu.make_async_remote_copy(
            src_ref=send.at[pl.ds(base, half)],
            dst_ref=recv.at[pl.ds(base, half)],
            send_sem=ssem.at[p, s],
            recv_sem=rsem.at[p, s],
            device_id=device,
            device_id_type=MESH,
        )
        copy.start()
        sent.append(copy)
        return copy

    def finish(s, p, copy):
        half = part_rows >> (s + 1)
        base = p * part_rows + part_rows - 2 * half
        keep = keeps[p][s]
        chunk = min(half, 4 * unit)
        copy.wait_recv()

        def add(i, carry):
            r = i * chunk
            mine = pl.ds(pl.multiple_of(keep + r, 16), chunk)
            acc[mine, :] = acc[mine, :] + recv[
                pl.ds(pl.multiple_of(base + r, 16), chunk), :
            ].astype(jnp.float32)
            return carry

        lax.fori_loop(0, half // chunk, add, 0)
        offs[p] = keep

    def spread(s, p):
        _, device = partner_of(orders[p][s])
        half = part_rows >> (s + 1)
        mine = pl.ds(pl.multiple_of(keeps[p][s], 16), half)
        copy = pltpu.make_async_remote_copy(
            src_ref=out.at[mine],
            dst_ref=out.at[mine],
            send_sem=ssem.at[p, stages + s],
            recv_sem=rsem.at[p, stages + s],
            device_id=device,
            device_id_type=MESH,
        )
        copy.start()
        sent.append(copy)
        return copy

    flight = [start(0, p) for p in range(3)]
    for s in range(stages):
        for p in range(3):
            finish(s, p, flight[p])
            if s + 1 < stages:
                flight[p] = start(s + 1, p)
            else:
                mine = pl.ds(pl.multiple_of(offs[p], 16), unit)
                out[mine, :] = acc[mine, :].astype(jnp.bfloat16)
                flight[p] = spread(stages - 1, p)
    for s in range(stages - 2, -1, -1):
        for p in range(3):
            flight[p].wait_recv()
            flight[p] = spread(s, p)
    for p in range(3):
        flight[p].wait_recv()
    for copy in sent:
        copy.wait_send()
    exchange_finish(edges, cells, side, ends, corner, halo_ssem, halo_rsem, sizes)


def summed(edges, cells, inner, outer, down, small, mesh_shape):
    orders, rows, devices = place(mesh_shape)
    stages = len(orders[0])
    return pl.pallas_call(
        partial(sum_kernel_body, orders, devices, (mesh_shape["lon"], mesh_shape["lat"])),
        name="sum_gradients",
        out_shape=[jax.ShapeDtypeStruct((rows, 256), jnp.bfloat16)] + halo_shapes(cells),
        in_specs=[VMEM_SPEC] * 6,
        out_specs=[VMEM_SPEC] * 4,
        scratch_shapes=[
            pltpu.VMEM((rows, 256), jnp.float32),
            pltpu.VMEM((rows, 256), jnp.bfloat16),
            pltpu.VMEM((rows, 256), jnp.bfloat16),
            pltpu.SemaphoreType.DMA((3, 2 * stages)),
            pltpu.SemaphoreType.DMA((3, 2 * stages)),
            pltpu.SemaphoreType.DMA((8,)),
            pltpu.SemaphoreType.DMA((8,)),
        ],
        compiler_params=pltpu.CompilerParams(
            collective_id=1, has_side_effects=True, vmem_limit_bytes=48 << 20
        ),
    )(edges, cells, inner, outer, down, small)


def finish_body(
    sums, cells, side, ends, corner, kernel, grad_cells,
    inner, outer, down, small, grad_field, wide, shifted,
):
    def squares(i, total):
        v = sums[pl.ds(pl.multiple_of(i * 64, 64), 64), :].astype(jnp.float32)
        v = v * v
        for width in (32, 16, 8):
            v = v[:width] + v[width:]
        return total + v

    total = jnp.sum(lax.fori_loop(0, 65, squares, jnp.zeros((8, 256), jnp.float32)))
    total = jnp.full((1, 256), total, jnp.float32)
    factor = jnp.minimum(1.0, math.sqrt(PARAMS) / jnp.sqrt(total + EPS))

    def write_inner(i, carry):
        r = pl.multiple_of(i * 64, 64)
        for c in range(4):
            inner[pl.ds(r, 64), c * 256 : (c + 1) * 256] = (
                sums[pl.ds(c * 256 + r, 64), :].astype(jnp.float32) * factor
            )
        return carry

    lax.fori_loop(0, 4, write_inner, 0)

    def write_rest(i, carry):
        r = pl.multiple_of(i * 64, 64)
        outer[pl.ds(r, 64), :] = sums[pl.ds(1024 + r, 64), :].astype(jnp.float32) * factor
        down[pl.ds(r, 64), 0:256] = sums[pl.ds(2048 + r, 64), :].astype(jnp.float32) * factor
        down[pl.ds(r, 64), 256:512] = sums[pl.ds(3072 + r, 64), :].astype(jnp.float32) * factor
        return carry

    lax.fori_loop(0, 16, write_rest, 0)
    small[...] = sums[4096:4160, :].astype(jnp.float32) * factor
    rows, cols, channels = cells.shape
    extend(cells, side, ends, corner, wide, shifted)

    def convolve(t, carry):
        first = t * 8
        here = pl.ds(pl.multiple_of(first * cols, 128), 8 * cols)
        out = spread_rows(shifted, kernel, first, 8, True).reshape(8 * cols, channels)
        grad_field[here, :] = (grad_cells[here, :].astype(jnp.float32) + out).astype(jnp.bfloat16)
        return carry

    lax.fori_loop(0, rows // 8, convolve, 0)


def finished(sums, cells, halos, kernel, grad_cells):
    rows, cols, channels = cells.shape
    f32 = jnp.float32
    shapes = ((256, 1024), (1024, 256), (1024, 512), (64, 256))
    return pl.pallas_call(
        finish_body,
        name="finish",
        out_shape=[jax.ShapeDtypeStruct(shape, f32) for shape in shapes]
        + [jax.ShapeDtypeStruct(grad_cells.shape, jnp.bfloat16)],
        in_specs=[VMEM_SPEC] * 7,
        out_specs=[VMEM_SPEC] * 5,
        scratch_shapes=[
            pltpu.VMEM((2, (rows + 6) * 32, channels // 2), f32),
            pltpu.VMEM((7, rows + 6, cols, channels), f32),
        ],
        compiler_params=pltpu.CompilerParams(vmem_limit_bytes=48 << 20),
    )(sums, cells, *halos, kernel, grad_cells)


def body(
    mesh_shape,
    field,
    depth_kernel,
    layer_norm_gain,
    inner_weight,
    outer_weight,
    layer_scale,
    down_weight,
    cotangent,
):
    _, rows, cols, channels = field.shape
    cells = field[0]
    edges = jnp.concatenate([cells[:, :3], cells[:, cols - 3 :]], axis=1).transpose(1, 0, 2)
    kernel = depth_kernel.reshape(49, channels)
    halos = halo(edges, cells, mesh_shape)
    coarse, grad_cells, grad_depth, grad_edges, raw_inner, raw_outer, raw_down, small = block(
        cells,
        halos,
        kernel,
        layer_norm_gain[None],
        inner_weight,
        outer_weight,
        layer_scale[None],
        down_weight,
        cotangent.reshape(-1, cotangent.shape[3]),
    )
    sums, *grad_halos = summed(
        grad_edges, grad_depth, raw_inner, raw_outer, raw_down, small, mesh_shape
    )
    grad_inner, grad_outer, grad_down, grad_small, grad_field = finished(
        sums, grad_depth, grad_halos, kernel, grad_cells
    )
    return (
        coarse.reshape(cotangent.shape),
        grad_field.reshape(field.shape),
        grad_small[:49].reshape(7, 7, channels),
        grad_small[49],
        grad_inner,
        grad_outer,
        grad_small[50],
        grad_down,
    )


def solution(mesh):
    return jax.shard_map(
        partial(body, dict(mesh.shape)),
        mesh=mesh,
        in_specs=(
            P(None, "lat", "lon", None),
            P(),
            P(),
            P(),
            P(),
            P(),
            P(),
            P(None, "lat", "lon", None),
        ),
        out_specs=(
            P(None, "lat", "lon", None),
            P(None, "lat", "lon", None),
            P(),
            P(),
            P(),
            P(),
            P(),
            P(),
        ),
        check_vma=False,
    )
```

```python
from functools import partial
import math

import jax
import jax.numpy as jnp
from jax import lax
from jax.experimental import pallas as pl
from jax.experimental.pallas import tpu as pltpu
from jax.sharding import PartitionSpec as P

PARAMS = 1061632


EPS = 1e-06


MESH = pl.DeviceIdType.MESH


def exchange_copies(edges, cells, side, ends, corner, ssem, rsem, sizes):
    lon, lat = lax.axis_index("lon"), lax.axis_index("lat")
    nlon, _ = sizes
    rows = cells.shape[0]
    left = lax.rem(lon + nlon - 1, nlon)
    right = lax.rem(lon + 1, nlon)

    def copy(src, dst, n, where):
        return pltpu.make_async_remote_copy(
            src_ref=src,
            dst_ref=dst,
            send_sem=ssem.at[n],
            recv_sem=rsem.at[n],
            device_id=where,
            device_id_type=MESH,
        )

    across = [
        copy(edges.at[0:3], side.at[1], 0, {"lon": left, "lat": lat}),
        copy(edges.at[3:6], side.at[0], 1, {"lon": right, "lat": lat}),
    ]
    above = lat - 1
    below = lat + 1
    up = [
        copy(cells.at[0:3], ends.at[1], 2, {"lon": lon, "lat": above}),
        copy(edges.at[0:3, 0:16], corner.at[1, 1], 3, {"lon": left, "lat": above}),
        copy(edges.at[3:6, 0:16], corner.at[1, 0], 4, {"lon": right, "lat": above}),
    ]
    down = [
        copy(cells.at[rows - 3 : rows], ends.at[0], 5, {"lon": lon, "lat": below}),
        copy(edges.at[0:3, rows - 16 : rows], corner.at[0, 1], 6, {"lon": left, "lat": below}),
        copy(edges.at[3:6, rows - 16 : rows], corner.at[0, 0], 7, {"lon": right, "lat": below}),
    ]
    return across, up, down


def greet(barrier, sizes):
    lon, lat = lax.axis_index("lon"), lax.axis_index("lat")
    nlon, nlat = sizes
    left = lax.rem(lon + nlon - 1, nlon)
    right = lax.rem(lon + 1, nlon)

    def signal(where):
        pl.semaphore_signal(barrier, inc=1, device_id=where, device_id_type=MESH)

    signal({"lon": left, "lat": lat})
    signal({"lon": right, "lat": lat})
    for there, ok in ((lat - 1, lat > 0), (lat + 1, lat < nlat - 1)):

        @pl.when(ok)
        def _():
            for other in (left, lon, right):
                signal({"lon": other, "lat": there})


def await_greetings(barrier, sizes, extra):
    lat = lax.axis_index("lat")
    beside = jnp.minimum(lat, 1) + jnp.minimum(sizes[1] - 1 - lat, 1)
    pl.semaphore_wait(barrier, 2 + extra + 3 * beside)


def exchange_start(edges, cells, side, ends, corner, ssem, rsem, sizes):
    lat = lax.axis_index("lat")
    across, up, down = exchange_copies(edges, cells, side, ends, corner, ssem, rsem, sizes)
    for c in across:
        c.start()

    @pl.when(lat > 0)
    def _():
        for c in up:
            c.start()

    @pl.when(lat < sizes[1] - 1)
    def _():
        for c in down:
            c.start()


def exchange_finish(edges, cells, side, ends, corner, ssem, rsem, sizes):
    lat = lax.axis_index("lat")
    across, up, down = exchange_copies(edges, cells, side, ends, corner, ssem, rsem, sizes)
    for c in across:
        c.wait()

    @pl.when(lat > 0)
    def _():
        for sent, came in zip(up, down):
            sent.wait_send()
            came.wait_recv()

    @pl.when(lat < sizes[1] - 1)
    def _():
        for sent, came in zip(down, up):
            sent.wait_send()
            came.wait_recv()

    @pl.when(lat == 0)
    def _():
        ends[0] = jnp.zeros(ends.shape[1:], ends.dtype)
        corner[0] = jnp.zeros(corner.shape[1:], corner.dtype)

    @pl.when(lat == sizes[1] - 1)
    def _():
        ends[1] = jnp.zeros(ends.shape[1:], ends.dtype)
        corner[1] = jnp.zeros(corner.shape[1:], corner.dtype)


def halo_body(sizes, edges, cells, side, ends, corner, ssem, rsem):
    barrier = pltpu.get_barrier_semaphore()
    greet(barrier, sizes)
    await_greetings(barrier, sizes, 0)
    exchange_start(edges, cells, side, ends, corner, ssem, rsem, sizes)
    exchange_finish(edges, cells, side, ends, corner, ssem, rsem, sizes)


def halo_shapes(cells):
    rows, cols, channels = cells.shape
    return [
        jax.ShapeDtypeStruct((2, 3, rows, channels), jnp.bfloat16),
        jax.ShapeDtypeStruct((2, 3, cols, channels), jnp.bfloat16),
        jax.ShapeDtypeStruct((2, 2, 3, 16, channels), jnp.bfloat16),
    ]


HALVES = (slice(0, 128), slice(128, 256))
VMEM_SPEC = pl.BlockSpec(memory_space=pltpu.VMEM)


def halo(edges, cells, mesh_shape):
    return pl.pallas_call(
        partial(halo_body, (mesh_shape["lon"], mesh_shape["lat"])),
        name="field_halo",
        cost_estimate=pl.CostEstimate(flops=0, bytes_accessed=16 << 20, transcendentals=0),
        out_shape=halo_shapes(cells),
        in_specs=[VMEM_SPEC] * 2,
        out_specs=[VMEM_SPEC] * 3,
        scratch_shapes=[pltpu.SemaphoreType.DMA((8,)), pltpu.SemaphoreType.DMA((8,))],
        compiler_params=pltpu.CompilerParams(
            collective_id=0, has_side_effects=True, vmem_limit_bytes=8 << 20
        ),
    )(edges, cells)


def extend(cells, side, ends, corner, wide, shifted):
    rows, cols, _ = cells.shape
    f32 = jnp.float32

    def put(where, values):
        values = values.astype(f32)
        for h in range(2):
            wide[h, where, :] = values[:, HALVES[h]]

    def fill(r, carry):
        put(pl.ds(pl.multiple_of((3 + r) * 32 + 8, 8), cols), cells[r])
        return carry

    lax.fori_loop(0, rows, fill, 0)
    for r in range(3):
        put(pl.ds(r * 32 + 8, cols), ends[0, r])
        put(pl.ds((rows + 3 + r) * 32 + 8, cols), ends[1, r])
    for h in range(2):
        for s, first in ((0, 5), (1, 8 + cols)):
            for c in range(3):
                column = first + c
                wide[h, pl.ds(3 * 32 + column, rows, stride=32), :] = side[
                    s, c, :, HALVES[h]
                ].astype(f32)
    for s, first in ((0, 5), (1, 8 + cols)):
        for c in range(3):
            high = corner[0, s, c].astype(f32)
            low = corner[1, s, c].astype(f32)
            for r in range(3):
                put(pl.ds(r * 32 + first + c, 1), high[13 + r : 14 + r])
                put(pl.ds((rows + 3 + r) * 32 + first + c, 1), low[r : r + 1])

    def shift(r, carry):
        for h in range(2):
            v = wide[h, pl.ds(pl.multiple_of(r * 32, 32), 32), :]
            for q in range(7):
                shifted[q, r, :, HALVES[h]] = pltpu.roll(v, 27 - q, 0)[:cols]
        return carry

    lax.fori_loop(0, rows + 6, shift, 0)


def spread_rows(shifted, kernel, first, count, flip):
    total = None
    for q in range(7):
        for p in range(7):
            at = (6 - p) * 7 + (6 - q) if flip else p * 7 + q
            term = shifted[q, pl.ds(first + p, count)] * kernel[at : at + 1, :]
            total = term if total is None else total + term
    return total


def dot(a, b, contract):
    return lax.dot_general(a, b, ((contract[0:1], contract[1:2]), ((), ())), preferred_element_type=jnp.float32)


def block_body(
    cells, side, ends, corner, kernel, gain, scale, inner, outer, down, cotangent,
    coarse, grad_cells, grad_depth, grad_edges, packed,
    wide, shifted, mixed, grad_wide, blocked, normed, hidden, grad_pre, grad_branch, terms,
):
    extend(cells, side, ends, corner, wide, shifted)
    rows, cols, channels = cells.shape
    f32, bf16 = jnp.float32, jnp.bfloat16
    cot = cotangent[...]
    pair = cols // 2
    for p in range(2):
        for q in range(2):
            at = (2 * p + q) * channels
            gp = dot(cot, down[at : at + channels, :], (1, 1)).astype(bf16).astype(f32)
            for i in range(rows // 2):
                first = (2 * i + p) * cols + q
                for lane in range(2):
                    grad_wide[lane, pl.ds(first, pair, stride=2), :] = gp[i * pair : (i + 1) * pair, HALVES[lane]]

    def convolve(t, carry):
        first = t * 8
        out = spread_rows(shifted, kernel, first, 8, False)
        mixed[pl.ds(pl.multiple_of(first * cols, 128), 8 * cols), :] = out.reshape(8 * cols, channels)
        return carry

    lax.fori_loop(0, rows // 8, convolve, 0)

    small = packed.at[4096:4160]
    packed[4096:, :] = jnp.zeros((packed.shape[0] - 4096, channels), f32)
    chunk = 16 * cols
    g = gain[...]
    ls = scale[...]

    def step(t, carry):
        raw_gain, raw_scale = carry
        here = pl.ds(pl.multiple_of(t * chunk, chunk), chunk)
        m = mixed[here, :]
        centered = m - jnp.mean(m, axis=-1, keepdims=True)
        inv = lax.rsqrt(jnp.mean(centered * centered, axis=-1, keepdims=True) + EPS)
        xhat = centered * inv
        nrm = (xhat * g).astype(bf16)
        normed[here, :] = nrm
        pre = dot(nrm, inner[...], (1, 0))
        cdf = 0.5 * (1.0 + lax.erf(pre * math.sqrt(0.5)))
        slope = cdf + pre * (jnp.exp(-0.5 * pre * pre) * (1.0 / math.sqrt(2.0 * math.pi)))
        hid = (pre * cdf).astype(bf16)
        hidden[here, :] = hid
        branch = dot(hid, outer[...], (1, 0))
        field = cells[pl.ds(t * 16, 16)].astype(f32).reshape(chunk, channels)
        block_out = (field + ls * branch).astype(bf16).astype(f32)
        for h in range(2):
            blocked[h, here, :] = block_out[:, HALVES[h]]
        gb = jnp.concatenate([grad_wide[h, here, :] for h in range(2)], axis=1)
        grad_cells[here, :] = gb.astype(bf16)
        raw_scale = raw_scale + jnp.sum(gb * branch, axis=0, keepdims=True)
        gbr = (gb * ls).astype(bf16)
        grad_branch[here, :] = gbr
        gp = (dot(gbr, outer[...], (1, 1)) * slope).astype(bf16)
        grad_pre[here, :] = gp
        gn = dot(gp, inner[...], (1, 1))
        raw_gain = raw_gain + jnp.sum(gn * xhat, axis=0, keepdims=True)
        gx = gn * g
        m1 = jnp.mean(gx, axis=-1, keepdims=True)
        m2 = jnp.mean(gx * xhat, axis=-1, keepdims=True)
        gd = ((gx - m1 - xhat * m2) * inv).astype(bf16)
        grad_depth[pl.ds(t * 16, 16)] = gd.reshape(16, cols, channels)
        gd = gd.astype(f32)
        mixed[here, :] = gd
        for h in range(2):
            grad_wide[h, here, :] = gd[:, HALVES[h]]
        return raw_gain, raw_scale

    zero = jnp.zeros((1, channels), f32)
    raw_gain, raw_scale = lax.fori_loop(0, rows // 16, step, (zero, zero))
    small[49:50, :] = raw_gain
    small[50:51, :] = raw_scale
    packed[1024:2048, :] = dot(hidden[...], grad_branch[...], (0, 0))
    for c in range(4):
        lanes = slice(c * 256, (c + 1) * 256)
        packed[lanes, :] = dot(normed[...], grad_pre[:, lanes], (0, 0))
    total = None
    for p in range(2):
        for q in range(2):
            at = (2 * p + q) * channels
            lanes = []
            for h in range(2):
                lanes.append(
                    jnp.concatenate(
                        [
                            blocked[h, pl.ds((2 * i + p) * cols + q, pair, stride=2), :]
                            for i in range(rows // 2)
                        ]
                    ).astype(bf16)
                )
            patch = jnp.concatenate(lanes, axis=1)
            part = dot(patch, down[at : at + channels, :], (1, 0))
            total = part if total is None else total + part
            raw = dot(patch, cot, (0, 0))
            packed[2048 + at : 2048 + at + channels, :] = raw[:, 0:256]
            packed[3072 + at : 3072 + at + channels, :] = raw[:, 256:512]
    coarse[...] = total.astype(bf16)

    terms[...] = jnp.zeros(terms.shape, f32)

    def kernel_step(t, carry):
        first = t * 4
        gd = mixed[pl.ds(pl.multiple_of(first * cols, 64), 4 * cols), :].reshape(4, cols, channels)
        for q in range(7):
            for p in range(7):
                prod = shifted[q, pl.ds(first + p, 4)] * gd
                prod = (prod[0] + prod[1]) + (prod[2] + prod[3])
                terms[p * 7 + q] = terms[p * 7 + q] + (prod[0:8] + prod[8:16])
        return carry

    lax.fori_loop(0, rows // 4, kernel_step, 0)
    small[0:49, :] = jnp.sum(terms[...], axis=1)
    for h in range(2):
        for c in range(3):
            for at, column in ((c, c), (3 + c, cols - 3 + c)):
                grad_edges[at, :, HALVES[h]] = grad_wide[
                    h, pl.ds(column, rows, stride=cols), :
                ].astype(bf16)


def block(cells, halos, kernel, gain, scale, inner, outer, down, cotangent, packed_rows):
    rows, cols, channels = cells.shape
    count = rows * cols
    hid = inner.shape[1]
    f32, bf16 = jnp.float32, jnp.bfloat16
    return pl.pallas_call(
        block_body,
        name="block",
        cost_estimate=pl.CostEstimate(flops=0, bytes_accessed=32 << 20, transcendentals=0),
        out_shape=[
            jax.ShapeDtypeStruct(cotangent.shape, bf16),
            jax.ShapeDtypeStruct((count, channels), bf16),
            jax.ShapeDtypeStruct(cells.shape, bf16),
            jax.ShapeDtypeStruct((6, rows, channels), bf16),
            jax.ShapeDtypeStruct((packed_rows, channels), f32),
        ],
        in_specs=[VMEM_SPEC] * 11,
        out_specs=[VMEM_SPEC] * 5,
        scratch_shapes=[
            pltpu.VMEM((2, (rows + 6) * 32, channels // 2), f32),
            pltpu.VMEM((7, rows + 6, cols, channels), f32),
            pltpu.VMEM((count, channels), f32),
            pltpu.VMEM((2, count, channels // 2), f32),
            pltpu.VMEM((2, count, channels // 2), f32),
            pltpu.VMEM((count, channels), bf16),
            pltpu.VMEM((count, hid), bf16),
            pltpu.VMEM((count, hid), bf16),
            pltpu.VMEM((count, channels), bf16),
            pltpu.VMEM((49, 8, channels), f32),
        ],
        compiler_params=pltpu.CompilerParams(vmem_limit_bytes=36 << 20),
    )(cells, *halos, kernel, gain, scale, inner, outer, down, cotangent)


def place(mesh_shape):
    lon_bits = mesh_shape["lon"].bit_length() - 1
    lat_bits = mesh_shape["lat"].bit_length() - 1
    core = [("lon", 0)]
    plane = [("lat", k) for k in range(lat_bits)] + [("lon", k) for k in range(1, min(2, lon_bits))]
    line = [("lon", k) for k in range(2, lon_bits)]
    orders = [
        [group for group in order if group]
        for order in ([core, line, plane], [core, plane, line], [core, plane, line])
    ]
    devices = mesh_shape["lon"] * mesh_shape["lat"]
    unit = 3 * 16 * devices
    rows = -(-(4096 + 64) // unit) * unit
    return orders, rows, devices


def peers_of(group):
    bits = [lax.rem(lax.div(lax.axis_index(axis), 2**k), 2) for axis, k in group]
    mine = sum(b * 2**n for n, b in enumerate(bits))
    peers = []
    for d in range(1, 2 ** len(group)):
        where = {"lon": lax.axis_index("lon"), "lat": lax.axis_index("lat")}
        index = mine
        for n, (axis, k) in enumerate(group):
            if d >> n & 1:
                where[axis] = where[axis] + (1 - 2 * bits[n]) * 2**k
                index = index + (1 - 2 * bits[n]) * 2**n
        peers.append((index, where))
    return mine, peers


def sum_kernel_body(
    orders, devices, sizes, edges, cells, packed,
    out, side, ends, corner, acc, send, recv, ssem, rsem, halo_ssem, halo_rsem,
):
    part_rows = acc.shape[0] // 3
    stages = len(orders[0])
    barrier = pltpu.get_barrier_semaphore()
    count = 0
    for group in orders[0]:
        for _, device in peers_of(group)[1]:
            pl.semaphore_signal(barrier, inc=1, device_id=device, device_id_type=MESH)
            count += 1
    greet(barrier, sizes)
    await_greetings(barrier, sizes, count)
    exchange_start(edges, cells, side, ends, corner, halo_ssem, halo_rsem, sizes)

    offs = [p * part_rows for p in range(3)]
    lens = [part_rows] * 3
    bases = [p * part_rows for p in range(3)]
    slots = [0] * 3
    owned = [[] for _ in range(3)]
    sent = []

    def piece(at, size):
        return pl.ds(pl.multiple_of(at, 16), size)

    def transfer(p, src, dst, device):
        copy = pltpu.make_async_remote_copy(
            src_ref=src,
            dst_ref=dst,
            send_sem=ssem.at[p, slots[p]],
            recv_sem=rsem.at[p, slots[p]],
            device_id=device,
            device_id_type=MESH,
        )
        copy.start()
        slots[p] += 1
        sent.append(copy)
        return copy

    def step_of(size):
        return next(n for n in (192, 128, 96, 64, 48, 32, 16) if size % n == 0)

    def start(s, p):
        mine, peers = peers_of(orders[p][s])
        size = lens[p] // (len(peers) + 1)
        source = packed if s == 0 else acc
        step = step_of(size)
        copies = []
        for n, (index, device) in enumerate(peers):
            base = bases[p] + n * size
            away = offs[p] + index * size

            def cast(i, carry):
                send[piece(base + i * step, step), :] = source[
                    piece(away + i * step, step), :
                ].astype(jnp.bfloat16)
                return carry

            lax.fori_loop(0, size // step, cast, 0)
            copies.append(
                transfer(p, send.at[pl.ds(base, size)], recv.at[pl.ds(base, size)], device)
            )
        return copies

    def finish(s, p, copies):
        mine, peers = peers_of(orders[p][s])
        size = lens[p] // (len(peers) + 1)
        base = bases[p]
        keep = offs[p] + mine * size
        source = packed if s == 0 else acc
        step = min(64, step_of(size))
        step = step if size % step == 0 else 16
        for copy in copies:
            copy.wait_recv()

        def add(i, carry):
            here = piece(keep + i * step, step)
            total = source[here, :]
            for n in range(len(peers)):
                total = total + recv[piece(base + n * size + i * step, step), :].astype(jnp.float32)
            if s + 1 < stages:
                acc[here, :] = total
            else:
                out[here, :] = total.astype(jnp.bfloat16)
            return carry

        lax.fori_loop(0, size // step, add, 0)
        owned[p].append((keep, size))
        bases[p] += len(peers) * size
        offs[p], lens[p] = keep, size

    def spread(s, p):
        keep, size = owned[p][s]
        mine = piece(keep, size)
        return [
            transfer(p, out.at[mine], out.at[mine], device)
            for _, device in peers_of(orders[p][s])[1]
        ]

    flight = [start(0, p) for p in range(3)]
    for s in range(stages):
        for p in range(3):
            finish(s, p, flight[p])
            flight[p] = start(s + 1, p) if s + 1 < stages else spread(s, p)
    for s in range(stages - 2, -1, -1):
        for p in range(3):
            for copy in flight[p]:
                copy.wait_recv()
            flight[p] = spread(s, p)
    for p in range(3):
        for copy in flight[p]:
            copy.wait_recv()
    for copy in sent:
        copy.wait_send()
    exchange_finish(edges, cells, side, ends, corner, halo_ssem, halo_rsem, sizes)


def summed(edges, cells, packed, mesh_shape):
    orders, rows, devices = place(mesh_shape)
    copies = 2 * sum(2 ** len(group) - 1 for group in orders[0])
    return pl.pallas_call(
        partial(sum_kernel_body, orders, devices, (mesh_shape["lon"], mesh_shape["lat"])),
        name="sum_gradients",
        cost_estimate=pl.CostEstimate(flops=0, bytes_accessed=96 << 20, transcendentals=0),
        out_shape=[jax.ShapeDtypeStruct((rows, 256), jnp.bfloat16)] + halo_shapes(cells),
        in_specs=[VMEM_SPEC] * 3,
        out_specs=[VMEM_SPEC] * 4,
        scratch_shapes=[
            pltpu.VMEM((rows, 256), jnp.float32),
            pltpu.VMEM((rows, 256), jnp.bfloat16),
            pltpu.VMEM((rows, 256), jnp.bfloat16),
            pltpu.SemaphoreType.DMA((3, copies)),
            pltpu.SemaphoreType.DMA((3, copies)),
            pltpu.SemaphoreType.DMA((8,)),
            pltpu.SemaphoreType.DMA((8,)),
        ],
        compiler_params=pltpu.CompilerParams(
            collective_id=1, has_side_effects=True, vmem_limit_bytes=32 << 20
        ),
    )(edges, cells, packed)


def finish_body(
    sums, cells, side, ends, corner, kernel, grad_cells,
    inner, outer, down, small, grad_field, wide, shifted,
):
    def squares(i, total):
        v = sums[pl.ds(pl.multiple_of(i * 64, 64), 64), :].astype(jnp.float32)
        v = v * v
        for width in (32, 16, 8):
            v = v[:width] + v[width:]
        return total + v

    total = jnp.sum(lax.fori_loop(0, 65, squares, jnp.zeros((8, 256), jnp.float32)))
    total = jnp.full((1, 256), total, jnp.float32)
    factor = jnp.minimum(1.0, math.sqrt(PARAMS) / jnp.sqrt(total + EPS))

    def write_inner(i, carry):
        r = pl.multiple_of(i * 64, 64)
        for c in range(4):
            inner[pl.ds(r, 64), c * 256 : (c + 1) * 256] = (
                sums[pl.ds(c * 256 + r, 64), :].astype(jnp.float32) * factor
            )
        return carry

    lax.fori_loop(0, 4, write_inner, 0)

    def write_rest(i, carry):
        r = pl.multiple_of(i * 64, 64)
        outer[pl.ds(r, 64), :] = sums[pl.ds(1024 + r, 64), :].astype(jnp.float32) * factor
        down[pl.ds(r, 64), 0:256] = sums[pl.ds(2048 + r, 64), :].astype(jnp.float32) * factor
        down[pl.ds(r, 64), 256:512] = sums[pl.ds(3072 + r, 64), :].astype(jnp.float32) * factor
        return carry

    lax.fori_loop(0, 16, write_rest, 0)
    small[...] = sums[4096:4160, :].astype(jnp.float32) * factor
    rows, cols, channels = cells.shape
    extend(cells, side, ends, corner, wide, shifted)

    def convolve(t, carry):
        first = t * 8
        here = pl.ds(pl.multiple_of(first * cols, 128), 8 * cols)
        out = spread_rows(shifted, kernel, first, 8, True).reshape(8 * cols, channels)
        grad_field[here, :] = (grad_cells[here, :].astype(jnp.float32) + out).astype(jnp.bfloat16)
        return carry

    lax.fori_loop(0, rows // 8, convolve, 0)


def finished(sums, cells, halos, kernel, grad_cells):
    rows, cols, channels = cells.shape
    f32 = jnp.float32
    shapes = ((256, 1024), (1024, 256), (1024, 512), (64, 256))
    return pl.pallas_call(
        finish_body,
        name="finish",
        cost_estimate=pl.CostEstimate(flops=0, bytes_accessed=16 << 20, transcendentals=0),
        out_shape=[jax.ShapeDtypeStruct(shape, f32) for shape in shapes]
        + [jax.ShapeDtypeStruct(grad_cells.shape, jnp.bfloat16)],
        in_specs=[VMEM_SPEC] * 7,
        out_specs=[VMEM_SPEC] * 5,
        scratch_shapes=[
            pltpu.VMEM((2, (rows + 6) * 32, channels // 2), f32),
            pltpu.VMEM((7, rows + 6, cols, channels), f32),
        ],
        compiler_params=pltpu.CompilerParams(vmem_limit_bytes=32 << 20),
    )(sums, cells, *halos, kernel, grad_cells)


def body(
    mesh_shape,
    field,
    depth_kernel,
    layer_norm_gain,
    inner_weight,
    outer_weight,
    layer_scale,
    down_weight,
    cotangent,
):
    _, rows, cols, channels = field.shape
    cells = field[0]
    edges = jnp.concatenate([cells[:, :3], cells[:, cols - 3 :]], axis=1).transpose(1, 0, 2)
    kernel = depth_kernel.reshape(49, channels)
    halos = halo(edges, cells, mesh_shape)
    coarse, grad_cells, grad_depth, grad_edges, packed = block(
        cells,
        halos,
        kernel,
        layer_norm_gain[None],
        layer_scale[None],
        inner_weight,
        outer_weight,
        down_weight,
        cotangent.reshape(-1, cotangent.shape[3]),
        place(mesh_shape)[1],
    )
    sums, *grad_halos = summed(grad_edges, grad_depth, packed, mesh_shape)
    grad_inner, grad_outer, grad_down, grad_small, grad_field = finished(
        sums, grad_depth, grad_halos, kernel, grad_cells
    )
    return (
        coarse.reshape(cotangent.shape),
        grad_field.reshape(field.shape),
        grad_small[:49].reshape(7, 7, channels),
        grad_small[49],
        grad_inner,
        grad_outer,
        grad_small[50],
        grad_down,
    )


def solution(mesh):
    return jax.shard_map(
        partial(body, dict(mesh.shape)),
        mesh=mesh,
        in_specs=(
            P(None, "lat", "lon", None),
            P(),
            P(),
            P(),
            P(),
            P(),
            P(),
            P(None, "lat", "lon", None),
        ),
        out_specs=(
            P(None, "lat", "lon", None),
            P(None, "lat", "lon", None),
            P(),
            P(),
            P(),
            P(),
            P(),
            P(),
        ),
        check_vma=False,
    )
```

```python
from functools import partial
import math

import jax
import jax.numpy as jnp
from jax import lax
from jax.experimental import pallas as pl
from jax.experimental.pallas import tpu as pltpu
from jax.sharding import PartitionSpec as P

PARAMS = 1061632


EPS = 1e-06


MESH = pl.DeviceIdType.MESH


def exchange_copies(edges, cells, side, ends, corner, ssem, rsem, sizes):
    lon, lat = lax.axis_index("lon"), lax.axis_index("lat")
    nlon, _ = sizes
    rows = cells.shape[0]
    left = lax.rem(lon + nlon - 1, nlon)
    right = lax.rem(lon + 1, nlon)

    def copy(src, dst, n, where):
        return pltpu.make_async_remote_copy(
            src_ref=src,
            dst_ref=dst,
            send_sem=ssem.at[n],
            recv_sem=rsem.at[n],
            device_id=where,
            device_id_type=MESH,
        )

    across = [
        copy(edges.at[0:3], side.at[1], 0, {"lon": left, "lat": lat}),
        copy(edges.at[3:6], side.at[0], 1, {"lon": right, "lat": lat}),
    ]
    above = lat - 1
    below = lat + 1
    up = [
        copy(cells.at[0:3], ends.at[1], 2, {"lon": lon, "lat": above}),
        copy(edges.at[0:3, 0:16], corner.at[1, 1], 3, {"lon": left, "lat": above}),
        copy(edges.at[3:6, 0:16], corner.at[1, 0], 4, {"lon": right, "lat": above}),
    ]
    down = [
        copy(cells.at[rows - 3 : rows], ends.at[0], 5, {"lon": lon, "lat": below}),
        copy(edges.at[0:3, rows - 16 : rows], corner.at[0, 1], 6, {"lon": left, "lat": below}),
        copy(edges.at[3:6, rows - 16 : rows], corner.at[0, 0], 7, {"lon": right, "lat": below}),
    ]
    return across, up, down


def greet(barrier, sizes):
    lon, lat = lax.axis_index("lon"), lax.axis_index("lat")
    nlon, nlat = sizes
    left = lax.rem(lon + nlon - 1, nlon)
    right = lax.rem(lon + 1, nlon)

    def signal(where):
        pl.semaphore_signal(barrier, inc=1, device_id=where, device_id_type=MESH)

    signal({"lon": left, "lat": lat})
    signal({"lon": right, "lat": lat})
    for there, ok in ((lat - 1, lat > 0), (lat + 1, lat < nlat - 1)):

        @pl.when(ok)
        def _():
            for other in (left, lon, right):
                signal({"lon": other, "lat": there})


def await_greetings(barrier, sizes, extra):
    lat = lax.axis_index("lat")
    beside = jnp.minimum(lat, 1) + jnp.minimum(sizes[1] - 1 - lat, 1)
    pl.semaphore_wait(barrier, 2 + extra + 3 * beside)


def exchange_start(edges, cells, side, ends, corner, ssem, rsem, sizes):
    lat = lax.axis_index("lat")
    across, up, down = exchange_copies(edges, cells, side, ends, corner, ssem, rsem, sizes)
    for c in across:
        c.start()

    @pl.when(lat > 0)
    def _():
        for c in up:
            c.start()

    @pl.when(lat < sizes[1] - 1)
    def _():
        for c in down:
            c.start()


def exchange_finish(edges, cells, side, ends, corner, ssem, rsem, sizes):
    lat = lax.axis_index("lat")
    across, up, down = exchange_copies(edges, cells, side, ends, corner, ssem, rsem, sizes)
    for c in across:
        c.wait()

    @pl.when(lat > 0)
    def _():
        for sent, came in zip(up, down):
            sent.wait_send()
            came.wait_recv()

    @pl.when(lat < sizes[1] - 1)
    def _():
        for sent, came in zip(down, up):
            sent.wait_send()
            came.wait_recv()

    @pl.when(lat == 0)
    def _():
        ends[0] = jnp.zeros(ends.shape[1:], ends.dtype)
        corner[0] = jnp.zeros(corner.shape[1:], corner.dtype)

    @pl.when(lat == sizes[1] - 1)
    def _():
        ends[1] = jnp.zeros(ends.shape[1:], ends.dtype)
        corner[1] = jnp.zeros(corner.shape[1:], corner.dtype)


def halo_shapes(cells):
    rows, cols, channels = cells.shape
    return [
        jax.ShapeDtypeStruct((2, 3, rows, channels), jnp.bfloat16),
        jax.ShapeDtypeStruct((2, 3, cols, channels), jnp.bfloat16),
        jax.ShapeDtypeStruct((2, 2, 3, 16, channels), jnp.bfloat16),
    ]


HALVES = (slice(0, 128), slice(128, 256))
VMEM_SPEC = pl.BlockSpec(memory_space=pltpu.VMEM)
FAR_SPEC = pl.BlockSpec(memory_space=pltpu.HBM)


def fetched(far, near, sems):
    copies = [pltpu.make_async_copy(f, n, sems.at[k]) for k, (f, n) in enumerate(zip(far, near))]
    for copy in copies:
        copy.start()
    return copies


def put(wide, where, values):
    values = values.astype(jnp.float32)
    for h in range(2):
        wide[h, where, :] = values[:, HALVES[h]]


def fill_inside(cells, wide):
    rows, cols, _ = cells.shape

    def fill(r, carry):
        put(wide, pl.ds(pl.multiple_of((3 + r) * 32 + 8, 8), cols), cells[r])
        return carry

    lax.fori_loop(0, rows, fill, 0)


def extend(cells, side, ends, corner, wide, shifted):
    rows, cols, _ = cells.shape
    f32 = jnp.float32
    for r in range(3):
        put(wide, pl.ds(r * 32 + 8, cols), ends[0, r])
        put(wide, pl.ds((rows + 3 + r) * 32 + 8, cols), ends[1, r])
    for h in range(2):
        for s, first in ((0, 5), (1, 8 + cols)):
            for c in range(3):
                column = first + c
                wide[h, pl.ds(3 * 32 + column, rows, stride=32), :] = side[
                    s, c, :, HALVES[h]
                ].astype(f32)
    for s, first in ((0, 5), (1, 8 + cols)):
        for c in range(3):
            high = corner[0, s, c].astype(f32)
            low = corner[1, s, c].astype(f32)
            for r in range(3):
                put(wide, pl.ds(r * 32 + first + c, 1), high[13 + r : 14 + r])
                put(wide, pl.ds((rows + 3 + r) * 32 + first + c, 1), low[r : r + 1])

    def shift(r, carry):
        for h in range(2):
            v = wide[h, pl.ds(pl.multiple_of(r * 32, 32), 32), :]
            for q in range(7):
                shifted[q, r, :, HALVES[h]] = pltpu.roll(v, 27 - q, 0)[:cols]
        return carry

    lax.fori_loop(0, rows + 6, shift, 0)


def spread_rows(shifted, kernel, first, count, flip):
    total = None
    for q in range(7):
        for p in range(7):
            i, j = (6 - p, 6 - q) if flip else (p, q)
            term = shifted[q, pl.ds(first + p, count)] * kernel[i, j : j + 1, :]
            total = term if total is None else total + term
    return total


def dot(a, b, contract):
    return lax.dot_general(a, b, ((contract[0:1], contract[1:2]), ((), ())), preferred_element_type=jnp.float32)


def main_body(
    orders, devices, sizes,
    cells_far, kernel_far, gain_far, scale_far, inner_far, outer_far, down_far, cotangent_far,
    coarse, grad_cells, grad_depth, sums, grad_side, grad_ends, grad_corner,
    cells, kernel, gain, scale, inner, outer, down, cotangent, loads,
    edges, side, ends, corner, grad_edges, packed,
    wide, shifted, mixed, grad_wide, blocked, normed, hidden, grad_pre, grad_branch, terms,
    acc, send, recv, ssem, rsem, first_ssem, first_rsem, second_ssem, second_rsem,
):
    barrier = pltpu.get_barrier_semaphore()
    count = 0
    for group in orders[0]:
        for _, device in peers_of(group)[1]:
            pl.semaphore_signal(barrier, inc=1, device_id=device, device_id_type=MESH)
            count += 1
    greet(barrier, sizes)
    loading = fetched(
        (cells_far, kernel_far, gain_far, scale_far, cotangent_far, down_far, inner_far, outer_far),
        (cells, kernel, gain, scale, cotangent, down, inner, outer),
        loads,
    )
    rows, cols, channels = cells.shape
    f32, bf16 = jnp.float32, jnp.bfloat16
    loading[0].wait()
    fill_inside(cells, wide)
    for h in range(2):
        for c in range(3):
            for at, column in ((c, c), (3 + c, cols - 3 + c)):
                edges[at, :, HALVES[h]] = wide[
                    h, pl.ds(3 * 32 + 8 + column, rows, stride=32), :
                ].astype(bf16)
    await_greetings(barrier, sizes, count)
    exchange_start(edges, cells, side, ends, corner, first_ssem, first_rsem, sizes)
    for copy in loading[1:]:
        copy.wait()
    adding = sum_steps(orders, packed, sums, acc, send, recv, ssem, rsem)
    cot = cotangent[...]
    pair = cols // 2
    for p in range(2):
        for q in range(2):
            at = (2 * p + q) * channels
            gp = dot(cot, down[at : at + channels, :], (1, 1)).astype(bf16).astype(f32)
            for i in range(rows // 2):
                first = (2 * i + p) * cols + q
                for lane in range(2):
                    grad_wide[lane, pl.ds(first, pair, stride=2), :] = gp[i * pair : (i + 1) * pair, HALVES[lane]]

    exchange_finish(edges, cells, side, ends, corner, first_ssem, first_rsem, sizes)
    extend(cells, side, ends, corner, wide, shifted)

    def convolve(t, carry):
        first = t * 8
        out = spread_rows(shifted, kernel, first, 8, False)
        mixed[pl.ds(pl.multiple_of(first * cols, 128), 8 * cols), :] = out.reshape(8 * cols, channels)
        return carry

    lax.fori_loop(0, rows // 8, convolve, 0)

    small = packed.at[4096:4160]
    packed[4096:, :] = jnp.zeros((packed.shape[0] - 4096, channels), f32)
    chunk = 16 * cols
    g = gain[...]
    ls = scale[...]

    def step(t, carry):
        raw_gain, raw_scale = carry
        here = pl.ds(pl.multiple_of(t * chunk, chunk), chunk)
        m = mixed[here, :]
        centered = m - jnp.mean(m, axis=-1, keepdims=True)
        inv = lax.rsqrt(jnp.mean(centered * centered, axis=-1, keepdims=True) + EPS)
        xhat = centered * inv
        nrm = (xhat * g).astype(bf16)
        normed[here, :] = nrm
        pre = dot(nrm, inner[...], (1, 0))
        cdf = 0.5 * (1.0 + lax.erf(pre * math.sqrt(0.5)))
        slope = cdf + pre * (jnp.exp(-0.5 * pre * pre) * (1.0 / math.sqrt(2.0 * math.pi)))
        hid = (pre * cdf).astype(bf16)
        hidden[here, :] = hid
        branch = dot(hid, outer[...], (1, 0))
        field = cells[pl.ds(t * 16, 16)].astype(f32).reshape(chunk, channels)
        block_out = (field + ls * branch).astype(bf16).astype(f32)
        for h in range(2):
            blocked[h, here, :] = block_out[:, HALVES[h]]
        gb = jnp.concatenate([grad_wide[h, here, :] for h in range(2)], axis=1)
        grad_cells[here, :] = gb.astype(bf16)
        raw_scale = raw_scale + jnp.sum(gb * branch, axis=0, keepdims=True)
        gbr = (gb * ls).astype(bf16)
        grad_branch[here, :] = gbr
        gp = (dot(gbr, outer[...], (1, 1)) * slope).astype(bf16)
        grad_pre[here, :] = gp
        gn = dot(gp, inner[...], (1, 1))
        raw_gain = raw_gain + jnp.sum(gn * xhat, axis=0, keepdims=True)
        gx = gn * g
        m1 = jnp.mean(gx, axis=-1, keepdims=True)
        m2 = jnp.mean(gx * xhat, axis=-1, keepdims=True)
        gd = ((gx - m1 - xhat * m2) * inv).astype(bf16)
        grad_depth[pl.ds(t * 16, 16)] = gd.reshape(16, cols, channels)
        gd = gd.astype(f32)
        mixed[here, :] = gd
        for h in range(2):
            grad_wide[h, here, :] = gd[:, HALVES[h]]
        return raw_gain, raw_scale

    zero = jnp.zeros((1, channels), f32)
    raw_gain, raw_scale = lax.fori_loop(0, rows // 16, step, (zero, zero))
    small[49:50, :] = raw_gain
    small[50:51, :] = raw_scale
    for h in range(2):
        for c in range(3):
            for at, column in ((c, c), (3 + c, cols - 3 + c)):
                grad_edges[at, :, HALVES[h]] = grad_wide[
                    h, pl.ds(column, rows, stride=cols), :
                ].astype(bf16)
    exchange_start(
        grad_edges, grad_depth, grad_side, grad_ends, grad_corner, second_ssem, second_rsem, sizes
    )
    packed[1024:2048, :] = dot(hidden[...], grad_branch[...], (0, 0))
    for c in range(4):
        lanes = slice(c * 256, (c + 1) * 256)
        packed[lanes, :] = dot(normed[...], grad_pre[:, lanes], (0, 0))
    next(adding)
    total = None
    for p in range(2):
        for q in range(2):
            at = (2 * p + q) * channels
            lanes = []
            for h in range(2):
                lanes.append(
                    jnp.concatenate(
                        [
                            blocked[h, pl.ds((2 * i + p) * cols + q, pair, stride=2), :]
                            for i in range(rows // 2)
                        ]
                    ).astype(bf16)
                )
            patch = jnp.concatenate(lanes, axis=1)
            part = dot(patch, down[at : at + channels, :], (1, 0))
            total = part if total is None else total + part
            raw = dot(patch, cot, (0, 0))
            packed[2048 + at : 2048 + at + channels, :] = raw[:, 0:256]
            packed[3072 + at : 3072 + at + channels, :] = raw[:, 256:512]
    coarse[...] = total.astype(bf16)
    next(adding)

    terms[...] = jnp.zeros(terms.shape, f32)

    def kernel_step(t, carry):
        first = t * 4
        gd = mixed[pl.ds(pl.multiple_of(first * cols, 64), 4 * cols), :].reshape(4, cols, channels)
        for q in range(7):
            for p in range(7):
                prod = shifted[q, pl.ds(first + p, 4)] * gd
                prod = (prod[0] + prod[1]) + (prod[2] + prod[3])
                terms[p * 7 + q] = terms[p * 7 + q] + (prod[0:8] + prod[8:16])
        return carry

    lax.fori_loop(0, rows // 4, kernel_step, 0)
    small[0:49, :] = jnp.sum(terms[...], axis=1)
    next(adding)
    for _ in adding:
        pass
    exchange_finish(
        grad_edges, grad_depth, grad_side, grad_ends, grad_corner, second_ssem, second_rsem, sizes
    )


def main(cells, kernel, gain, scale, inner, outer, down, cotangent, mesh_shape):
    rows, cols, channels = cells.shape
    count = rows * cols
    hid = inner.shape[1]
    f32, bf16 = jnp.float32, jnp.bfloat16
    orders, packed_rows, devices = place(mesh_shape)
    copies = 2 * sum(2 ** len(group) - 1 for group in orders[0])
    operands = (cells, kernel, gain, scale, inner, outer, down, cotangent)
    sizes = (mesh_shape["lon"], mesh_shape["lat"])
    return pl.pallas_call(
        partial(main_body, orders, devices, sizes),
        name="main",
        out_shape=[
            jax.ShapeDtypeStruct(cotangent.shape, bf16),
            jax.ShapeDtypeStruct((count, channels), bf16),
            jax.ShapeDtypeStruct(cells.shape, bf16),
            jax.ShapeDtypeStruct((packed_rows, channels), bf16),
        ]
        + halo_shapes(cells),
        in_specs=[FAR_SPEC] * 8,
        out_specs=[VMEM_SPEC] * 7,
        scratch_shapes=[pltpu.VMEM(x.shape, x.dtype) for x in operands]
        + [
            pltpu.SemaphoreType.DMA((8,)),
            pltpu.VMEM((6, rows, channels), bf16),
        ]
        + [pltpu.VMEM(x.shape, x.dtype) for x in halo_shapes(cells)]
        + [
            pltpu.VMEM((6, rows, channels), bf16),
            pltpu.VMEM((packed_rows, channels), f32),
            pltpu.VMEM((2, (rows + 6) * 32, channels // 2), f32),
            pltpu.VMEM((7, rows + 6, cols, channels), f32),
            pltpu.VMEM((count, channels), f32),
            pltpu.VMEM((2, count, channels // 2), f32),
            pltpu.VMEM((2, count, channels // 2), f32),
            pltpu.VMEM((count, channels), bf16),
            pltpu.VMEM((count, hid), bf16),
            pltpu.VMEM((count, hid), bf16),
            pltpu.VMEM((count, channels), bf16),
            pltpu.VMEM((49, 8, channels), f32),
            pltpu.VMEM((packed_rows, channels), f32),
            pltpu.VMEM((packed_rows, channels), bf16),
            pltpu.VMEM((packed_rows, channels), bf16),
            pltpu.SemaphoreType.DMA((3, copies)),
            pltpu.SemaphoreType.DMA((3, copies)),
        ]
        + [pltpu.SemaphoreType.DMA((8,))] * 4,
        compiler_params=pltpu.CompilerParams(
            collective_id=0, has_side_effects=True, vmem_limit_bytes=58 << 20
        ),
    )(*operands)


def place(mesh_shape):
    lon_bits = mesh_shape["lon"].bit_length() - 1
    lat_bits = mesh_shape["lat"].bit_length() - 1
    core = [("lon", 0)]
    plane = [("lat", k) for k in range(lat_bits)] + [("lon", k) for k in range(1, min(2, lon_bits))]
    line = [("lon", k) for k in range(2, lon_bits)]
    orders = [
        [group for group in order if group]
        for order in ([core, line, plane], [core, plane, line], [core, plane, line])
    ]
    devices = mesh_shape["lon"] * mesh_shape["lat"]
    unit = 3 * 16 * devices
    rows = -(-(4096 + 64) // unit) * unit
    return orders, rows, devices


def peers_of(group):
    bits = [lax.rem(lax.div(lax.axis_index(axis), 2**k), 2) for axis, k in group]
    mine = sum(b * 2**n for n, b in enumerate(bits))
    peers = []
    for d in range(1, 2 ** len(group)):
        where = {"lon": lax.axis_index("lon"), "lat": lax.axis_index("lat")}
        index = mine
        for n, (axis, k) in enumerate(group):
            if d >> n & 1:
                where[axis] = where[axis] + (1 - 2 * bits[n]) * 2**k
                index = index + (1 - 2 * bits[n]) * 2**n
        peers.append((index, where))
    return mine, peers


def sum_steps(orders, packed, out, acc, send, recv, ssem, rsem):
    part_rows = acc.shape[0] // 3
    stages = len(orders[0])
    offs = [p * part_rows for p in range(3)]
    lens = [part_rows] * 3
    bases = [p * part_rows for p in range(3)]
    slots = [0] * 3
    owned = [[] for _ in range(3)]
    sent = []

    def piece(at, size):
        return pl.ds(pl.multiple_of(at, 16), size)

    def transfer(p, src, dst, device):
        copy = pltpu.make_async_remote_copy(
            src_ref=src,
            dst_ref=dst,
            send_sem=ssem.at[p, slots[p]],
            recv_sem=rsem.at[p, slots[p]],
            device_id=device,
            device_id_type=MESH,
        )
        copy.start()
        slots[p] += 1
        sent.append(copy)
        return copy

    def step_of(size):
        return next(n for n in (192, 128, 96, 64, 48, 32, 16) if size % n == 0)

    def start(s, p):
        mine, peers = peers_of(orders[p][s])
        size = lens[p] // (len(peers) + 1)
        source = packed if s == 0 else acc
        step = step_of(size)
        copies = []
        for n, (index, device) in enumerate(peers):
            base = bases[p] + n * size
            away = offs[p] + index * size

            def cast(i, carry):
                send[piece(base + i * step, step), :] = source[
                    piece(away + i * step, step), :
                ].astype(jnp.bfloat16)
                return carry

            lax.fori_loop(0, size // step, cast, 0)
            copies.append(
                transfer(p, send.at[pl.ds(base, size)], recv.at[pl.ds(base, size)], device)
            )
        return copies

    def finish(s, p, copies):
        mine, peers = peers_of(orders[p][s])
        size = lens[p] // (len(peers) + 1)
        base = bases[p]
        keep = offs[p] + mine * size
        source = packed if s == 0 else acc
        step = min(64, step_of(size))
        step = step if size % step == 0 else 16
        for copy in copies:
            copy.wait_recv()

        def add(i, carry):
            here = piece(keep + i * step, step)
            total = source[here, :]
            for n in range(len(peers)):
                total = total + recv[piece(base + n * size + i * step, step), :].astype(jnp.float32)
            if s + 1 < stages:
                acc[here, :] = total
            else:
                out[here, :] = total.astype(jnp.bfloat16)
            return carry

        lax.fori_loop(0, size // step, add, 0)
        owned[p].append((keep, size))
        bases[p] += len(peers) * size
        offs[p], lens[p] = keep, size

    def spread(s, p):
        keep, size = owned[p][s]
        mine = piece(keep, size)
        return [
            transfer(p, out.at[mine], out.at[mine], device)
            for _, device in peers_of(orders[p][s])[1]
        ]

    flight = []
    for p in range(3):
        flight.append(start(0, p))
        yield
    for s in range(stages):
        for p in range(3):
            finish(s, p, flight[p])
            flight[p] = start(s + 1, p) if s + 1 < stages else spread(s, p)
    for s in range(stages - 2, -1, -1):
        for p in range(3):
            for copy in flight[p]:
                copy.wait_recv()
            flight[p] = spread(s, p)
    for p in range(3):
        for copy in flight[p]:
            copy.wait_recv()
    for copy in sent:
        copy.wait_send()


def finish_body(
    sums_far, cells_far, side_far, ends_far, corner_far, kernel_far, grad_cells_far,
    inner, outer, down, grad_kernel, gain, scale, grad_field,
    sums, cells, side, ends, corner, kernel, grad_cells, loads, wide, shifted,
):
    loading = fetched(
        (cells_far, side_far, ends_far, corner_far, kernel_far, grad_cells_far, sums_far),
        (cells, side, ends, corner, kernel, grad_cells, sums),
        loads,
    )
    for copy in loading[:6]:
        copy.wait()
    fill_inside(cells, wide)
    extend(cells, side, ends, corner, wide, shifted)
    rows, cols, channels = cells.shape

    def convolve(t, carry):
        first = t * 8
        here = pl.ds(pl.multiple_of(first * cols, 128), 8 * cols)
        out = spread_rows(shifted, kernel, first, 8, True).reshape(8 * cols, channels)
        grad_field[here, :] = (grad_cells[here, :].astype(jnp.float32) + out).astype(jnp.bfloat16)
        return carry

    lax.fori_loop(0, rows // 8, convolve, 0)
    loading[6].wait()

    def squares(i, total):
        v = sums[pl.ds(pl.multiple_of(i * 64, 64), 64), :].astype(jnp.float32)
        v = v * v
        for width in (32, 16, 8):
            v = v[:width] + v[width:]
        return total + v

    total = jnp.sum(lax.fori_loop(0, 65, squares, jnp.zeros((8, 256), jnp.float32)))
    total = jnp.full((1, 256), total, jnp.float32)
    factor = jnp.minimum(1.0, math.sqrt(PARAMS) / jnp.sqrt(total + EPS))

    def write_inner(i, carry):
        r = pl.multiple_of(i * 64, 64)
        for c in range(4):
            inner[pl.ds(r, 64), c * 256 : (c + 1) * 256] = (
                sums[pl.ds(c * 256 + r, 64), :].astype(jnp.float32) * factor
            )
        return carry

    lax.fori_loop(0, 4, write_inner, 0)

    def write_rest(i, carry):
        r = pl.multiple_of(i * 64, 64)
        outer[pl.ds(r, 64), :] = sums[pl.ds(1024 + r, 64), :].astype(jnp.float32) * factor
        down[pl.ds(r, 64), 0:256] = sums[pl.ds(2048 + r, 64), :].astype(jnp.float32) * factor
        down[pl.ds(r, 64), 256:512] = sums[pl.ds(3072 + r, 64), :].astype(jnp.float32) * factor
        return carry

    lax.fori_loop(0, 16, write_rest, 0)
    last = sums[4096:4160, :].astype(jnp.float32) * factor
    for p in range(7):
        grad_kernel[p] = last[7 * p : 7 * p + 7]
    gain[...] = last[49:50]
    scale[...] = last[50:51]


def finished(sums, cells, halos, kernel, grad_cells):
    rows, cols, channels = cells.shape
    f32 = jnp.float32
    shapes = ((256, 1024), (1024, 256), (1024, 512), kernel.shape, (1, channels), (1, channels))
    operands = (sums, cells, *halos, kernel, grad_cells)
    return pl.pallas_call(
        finish_body,
        name="finish",
        out_shape=[jax.ShapeDtypeStruct(shape, f32) for shape in shapes]
        + [jax.ShapeDtypeStruct(grad_cells.shape, jnp.bfloat16)],
        in_specs=[FAR_SPEC] * 7,
        out_specs=[VMEM_SPEC] * 7,
        scratch_shapes=[pltpu.VMEM(x.shape, x.dtype) for x in operands]
        + [
            pltpu.SemaphoreType.DMA((7,)),
            pltpu.VMEM((2, (rows + 6) * 32, channels // 2), f32),
            pltpu.VMEM((7, rows + 6, cols, channels), f32),
        ],
        compiler_params=pltpu.CompilerParams(vmem_limit_bytes=58 << 20),
    )(*operands)


def body(
    mesh_shape,
    field,
    depth_kernel,
    layer_norm_gain,
    inner_weight,
    outer_weight,
    layer_scale,
    down_weight,
    cotangent,
):
    channels = field.shape[3]
    coarse, grad_cells, grad_depth, sums, *grad_halos = main(
        field[0],
        depth_kernel,
        layer_norm_gain[None],
        layer_scale[None],
        inner_weight,
        outer_weight,
        down_weight,
        cotangent.reshape(-1, cotangent.shape[3]),
        mesh_shape,
    )
    grad_inner, grad_outer, grad_down, grad_kernel, grad_gain, grad_scale, grad_field = finished(
        sums, grad_depth, grad_halos, depth_kernel, grad_cells
    )
    return (
        coarse.reshape(cotangent.shape),
        grad_field.reshape(field.shape),
        grad_kernel,
        grad_gain.reshape(channels),
        grad_inner,
        grad_outer,
        grad_scale.reshape(channels),
        grad_down,
    )


def solution(mesh):
    return jax.shard_map(
        partial(body, dict(mesh.shape)),
        mesh=mesh,
        in_specs=(
            P(None, "lat", "lon", None),
            P(),
            P(),
            P(),
            P(),
            P(),
            P(),
            P(None, "lat", "lon", None),
        ),
        out_specs=(
            P(None, "lat", "lon", None),
            P(None, "lat", "lon", None),
            P(),
            P(),
            P(),
            P(),
            P(),
            P(),
        ),
        check_vma=False,
    )
```
